32 devices in a mesh: gx: 16 (over z, x, core), gy: 2 (over y).
Axes of the slice: x: 2, y: 2, z: 4, core: 2. Of those that a mesh axis runs over, the one named last changes fastest.
Arguments:
- rhs: float32 [16, 2, 4, 320], P('gx', 'gy'), may hold values from -120 to 120
- vol_jac: float32 [16, 2, 4, 320, 320], P('gx', 'gy'), may hold values from -0.3125 to 0.3125
- inv_step: float32 [16, 2, 4], P('gx', 'gy'), may hold values from 4 to 16
- face_jac: float32 [16, 2, 4, 6, 5, 5], P('gx', 'gy'), may hold values from -1 to 1
- orientation: int32 [16, 2, 4, 6], P('gx', 'gy'), may hold values from 0 to 7, as said below
Outputs:
- newton_update: float32 [16, 2, 4, 320], P('gx', 'gy')
- residual_ratio: float32 [], replicated
The draws below stay inside these ranges and needn't reach their ends.
Inputs may be any that keep to these rules, and one draw needn't show every extreme that they name: `orientation`: the two sides of every face carry inverse codes: where one side has code o, the other has o if o < 4, else 4 + (o & 2) / 2 + 2 (o & 1).
All inputs are finite; a program needn't handle non-finite values.
Results may differ from the reference program's by a relative error of at most 0.0025.
Values sent between devices are 32-bit elements; how exact they have to be, the bound alone decides.
A program may use at most 256 MiB of HBM per device.

```python
import math
import jax
import jax.numpy as jnp
import numpy as np
from jax import lax

Q = 4
NV = 5
ITERS = 3
NS_STEPS = 3
NP = 64
BLK = 320
NX = 16
NY = 2
NZ = 4


def draw_rhs(key, part):
    noise_key, scale_key = jax.random.split(jax.random.fold_in(key, 11))
    full_shape = (NX, NY, NZ, BLK)
    ramp_first = jnp.arange(NX, dtype=jnp.float32)[:, None, None, None]
    ramp_second = jnp.arange(NY, dtype=jnp.float32)[None, :, None, None]
    position_ramp = 1.0 + 2.0 * (ramp_first + ramp_second) / (NX + NY - 2)
    noise_part = jax.random.truncated_normal(noise_key, -4.0, 4.0, full_shape, jnp.float32)
    spread = 10.0 ** jax.random.uniform(scale_key, (NX, NY, NZ, 1), jnp.float32, 0.0, 1.0)
    return noise_part * spread * position_ramp


def inverse_code(codes):
    swapped = 4 + codes // 2 % 2 + 2 * (codes % 2)
    return jnp.where(codes >= 4, swapped, codes)


def draw_orientation(key, part):
    upper_codes = jax.random.randint(jax.random.fold_in(key, 23), (NX, NY, NZ, 3), 0, 8, dtype=jnp.int32)
    sides = []
    for direction_id in range(3):
        upper_side = upper_codes[..., direction_id]
        lower_side = inverse_code(jnp.roll(upper_side, 1, axis=direction_id))
        sides.append(lower_side)
        sides.append(upper_side)
    return jnp.stack(sides, axis=-1).astype(jnp.int32)


def block_scale(key, dims, shards, low, high):
    level, own = 1.0, jax.random.fold_in(key, 6)
    for axis_at, parts in shards:
        heights = jnp.exp(jax.random.uniform(jax.random.fold_in(own, axis_at), (parts,), jnp.float32, low / len(shards), high / len(shards)))
        level = level * jnp.repeat(heights, dims[axis_at] // parts).reshape([-1 if axis == axis_at else 1 for axis in range(len(dims))])
    return level


def centred(rng, extent, scale, bound, cuts=(), held_as=jnp.bfloat16):
    result = scale * jax.random.normal(rng, extent, jnp.float32)
    if cuts:
        result = result * block_scale(rng, extent, cuts, -0.22, 0.18)
    return jnp.clip(result, -bound, bound).astype(held_as)


def setup_inputs(seed: int = 0) -> dict:
    key_list = jax.random.split(jax.random.key(seed), 6)
    return {
        "rhs": draw_rhs(jax.random.fold_in(key_list[5], 71), 0),
        "vol_jac": centred(key_list[1], (NX, NY, NZ, BLK, BLK), BLK ** -0.5, 0.3125, ((0, 16), (1, 2)), jnp.float32),
        "inv_step": jnp.clip(jnp.exp(math.log(16.0) - 1.3862944 * jax.random.uniform(key_list[2], (NX, NY, NZ), jnp.float32) ** block_scale(key_list[2], (NX, NY, NZ), ((0, 16), (1, 2)), -0.2, 0.2)), 4.0, 16.0),
        "face_jac": jnp.clip(jax.random.uniform(key_list[3], (NX, NY, NZ, 6, NV, NV), jnp.float32, -1.0, 1.0) * block_scale(key_list[3], (NX, NY, NZ, 6, NV, NV), ((0, 16), (1, 2)), -0.4, 0.0), -1.0, 1.0),
        "orientation": draw_orientation(jax.random.fold_in(key_list[5], 71), 0),
    }


penalty = 4.0
highest = lax.Precision.HIGHEST

def face_tables(nodes_side):
    node_count = nodes_side ** 3
    across = nodes_side * nodes_side
    selector = np.zeros((6, node_count, across), np.float32)
    for face_id in range(6):
        for node_id in range(node_count):
            first_coord = node_id % nodes_side
            second_coord = node_id // nodes_side % nodes_side
            third_coord = node_id // across
            fixed_axis = [first_coord, first_coord, second_coord, second_coord, third_coord, third_coord][face_id]
            target = 0 if face_id % 2 == 0 else nodes_side - 1
            if fixed_axis == target:
                plane_pair = [(second_coord, third_coord), (second_coord, third_coord), (first_coord, third_coord), (first_coord, third_coord), (first_coord, second_coord), (first_coord, second_coord)][face_id]
                selector[face_id, node_id, plane_pair[0] + nodes_side * plane_pair[1]] = 1.0
    turning = np.zeros((8, across, across), np.float32)
    for orient_code in range(8):
        for face_node in range(across):
            along_first = face_node % nodes_side
            along_second = face_node // nodes_side
            if orient_code & 4:
                along_first, along_second = (along_second, along_first)
            if orient_code & 1:
                along_first = nodes_side - 1 - along_first
            if orient_code & 2:
                along_second = nodes_side - 1 - along_second
            turning[orient_code, face_node, along_first + nodes_side * along_second] = 1.0
    return (selector, turning)

def element_traces(operand, selector):
    shaped = operand.reshape(operand.shape[:-1] + (NV, NP))
    return jnp.einsum('...vn,fnq->...fvq', shaped, selector, precision=highest)

def lift_faces(face_values, selector):
    lifted = jnp.einsum('...fvq,fnq->...vn', face_values, selector, precision=highest)
    return lifted.reshape(lifted.shape[:-2] + (NV * NP,))

def face_terms(own_traces, oriented, face_jac):
    identity = jnp.eye(NV, dtype=jnp.float32)
    own_part = jnp.einsum('...fij,...fjq->...fiq', face_jac + penalty * identity, own_traces, precision=highest)
    other_part = jnp.einsum('...fij,...fjq->...fiq', face_jac - penalty * identity, oriented, precision=highest)
    return 0.5 * (own_part + other_part)

def invert_blocks(vol_jac, inv_step, face_jac, selector):
    eye_nodes = jnp.eye(NP, dtype=jnp.float32)
    eye_block = jnp.eye(NV * NP, dtype=jnp.float32)
    coverage = lax.optimization_barrier(jnp.sum(selector, axis=-1))
    own_face = 0.5 * (face_jac + penalty * jnp.eye(NV, dtype=jnp.float32))
    node_part = jnp.einsum('...fij,fn->...ijn', own_face, coverage, precision=highest)
    face_block = jnp.einsum('...ijn,nm->...injm', node_part, eye_nodes, precision=highest)
    face_block = face_block.reshape(face_block.shape[:-4] + (NV * NP, NV * NP))
    element_block = vol_jac + face_block + inv_step[..., None, None] * eye_block
    diagonal = jnp.diagonal(element_block, axis1=-2, axis2=-1)
    approx = eye_block * (1.0 / diagonal)[..., :, None]
    for sweep_id in range(NS_STEPS):
        product = jnp.einsum('...rk,...kc->...rc', element_block, approx, precision=highest)
        approx = 2.0 * approx - jnp.einsum('...rk,...kc->...rc', approx, product, precision=highest)
    return approx

def apply_precond(precond, operand):
    return jnp.einsum('...rc,...c->...r', precond, operand, precision=highest)

def apply_jacobian(operand, vol_jac, inv_step, face_jac, orient_mats, selector):
    own_traces = element_traces(operand, selector)
    roll_moves = [(1, 0), (-1, 0), (1, 1), (-1, 1), (1, 2), (-1, 2)]
    gathered = []
    for face_id in range(6):
        shifted = jnp.roll(own_traces, roll_moves[face_id][0], axis=roll_moves[face_id][1])
        gathered.append(shifted[:, :, :, face_id ^ 1])
    neighbours = jnp.stack(gathered, axis=3)
    oriented = jnp.einsum('...fqp,...fvp->...fvq', orient_mats, neighbours, precision=highest)
    coupled = face_terms(own_traces, oriented, face_jac)
    volume = jnp.einsum('...rc,...c->...r', vol_jac, operand, precision=highest)
    return inv_step[..., None] * operand + volume + lift_faces(coupled, selector)

def least_squares(columns, initial_norm):
    steps_count = len(columns)
    rotations = []
    target_values = [initial_norm] + [jnp.zeros_like(initial_norm)] * steps_count
    upper_rows = []
    for column_id in range(steps_count):
        column = list(columns[column_id])
        for index_id in range(column_id):
            cosine, sine_part = rotations[index_id]
            top_value = cosine * column[index_id] + sine_part * column[index_id + 1]
            column[index_id + 1] = -sine_part * column[index_id] + cosine * column[index_id + 1]
            column[index_id] = top_value
        radius = jnp.sqrt(column[column_id] * column[column_id] + column[column_id + 1] * column[column_id + 1])
        cosine = column[column_id] / radius
        sine_part = column[column_id + 1] / radius
        rotations.append((cosine, sine_part))
        column[column_id] = radius
        target_values[column_id + 1] = -sine_part * target_values[column_id]
        target_values[column_id] = cosine * target_values[column_id]
        upper_rows.append(column)
    coefficients = [None] * steps_count
    for row_id in reversed(range(steps_count)):
        running = target_values[row_id]
        for later_id in range(row_id + 1, steps_count):
            running = running - upper_rows[later_id][row_id] * coefficients[later_id]
        coefficients[row_id] = running / upper_rows[row_id][row_id]
    return (coefficients, jnp.abs(target_values[steps_count]) / initial_norm)

def reference(rhs, vol_jac, inv_step, face_jac, orientation):
    selector_np, turning_np = face_tables(Q)
    selector = jnp.asarray(selector_np)
    turning = jnp.asarray(turning_np)

    def invert_slab(slab_args):
        return invert_blocks(slab_args[0], slab_args[1], slab_args[2], selector)
    precond = lax.map(invert_slab, (vol_jac, inv_step, face_jac))
    orient_hot = (orientation[..., None] == jnp.arange(8, dtype=jnp.int32)).astype(jnp.float32)
    orient_mats = jnp.einsum('...fo,oqp->...fqp', orient_hot, turning, precision=highest)
    initial_norm = jnp.sqrt(jnp.sum(rhs * rhs))
    krylov_basis = [rhs / initial_norm]
    directions = []
    columns = []
    for iteration in range(ITERS):
        direction = apply_precond(precond, krylov_basis[-1])
        directions.append(direction)
        image_vec = apply_jacobian(direction, vol_jac, inv_step, face_jac, orient_mats, selector)
        column = []
        for vector in krylov_basis:
            projection = jnp.sum(image_vec * vector)
            image_vec = image_vec - projection * vector
            column.append(projection)
        new_norm = jnp.sqrt(jnp.sum(image_vec * image_vec))
        column.append(new_norm)
        columns.append(column)
        krylov_basis.append(image_vec / new_norm)
    coefficients, residual_ratio = least_squares(columns, initial_norm)
    update = coefficients[0] * directions[0]
    for index_id in range(1, ITERS):
        update = update + coefficients[index_id] * directions[index_id]
    return (update, residual_ratio)
```

```python
import jax
import jax.numpy as jnp
from jax import lax
from jax.experimental import pallas as pl
from jax.experimental.pallas import tpu as pltpu
from jax.sharding import PartitionSpec as P

Q = 4
NV = 5
ITERS = 3
NS_STEPS = 3
NP = Q**3
BLK = NV * NP
FACES = 6
AXES = 3
PENALTY = 4.0
SWEEPS = 2**NS_STEPS - 1
MESH = pl.DeviceIdType.MESH
DOWN = 2.0**-40
TINY = 1e-36
UNROLL = 64


def iota(shape, dim):
    return lax.broadcasted_iota(jnp.int32, shape, dim)


def axis_coords(node, axis):
    first, second, third = node % Q, node // Q % Q, node // (Q * Q)
    pair = [(second, third), (first, third), (first, second)][axis]
    return [first, second, third][axis], pair[0], pair[1]


def node_of(axis, fixed, one, two):
    first, second, third = [(fixed, one, two), (one, fixed, two), (one, two, fixed)][axis]
    return first + Q * second + Q * Q * third


def kernel(
    nx, ny, nz,
    vol, rhs_in, face_in, step_in, orient_in,
    out, ratio,
    held_vol, rhs, face, inv_step, orient, mat, aux, wts, own, turn, dinv, basis, dirs, state, halo, packed,
    series, fourth, left_op, right_op,
    vol_sem, small_sem, halo_send, halo_recv, sum_send, sum_recv,
):
    gx, gy = lax.axis_index("gx"), lax.axis_index("gy")
    devices = nx * ny
    width = nz * NP
    pairs = nz // 2
    sides = 3 if ny == 2 else 4
    lanes = 2 * NP
    me = gx * ny + gy
    loads = [
        pltpu.make_async_copy(vol.at[0, 0, e], held_vol.at[e], vol_sem.at[e]) for e in range(nz)
    ]
    small = [
        pltpu.make_async_copy(source, target, small_sem.at[at])
        for at, (source, target) in enumerate(
            [(face_in, face), (orient_in, orient), (step_in, inv_step), (rhs_in, rhs)]
        )
    ]
    for load in small:
        load.start()
    for load in loads:
        load.start()

    def other(along, across):
        return lax.rem(gx + along, nx), lax.rem(gy + across, ny)

    def each_other(visit):
        if devices <= UNROLL:
            for step in range(1, devices):
                visit(step // ny, step % ny)
        else:
            def several(step, carry):
                visit(step // ny, step % ny)
                return carry

            lax.fori_loop(1, devices, several, 0)

    barrier = pltpu.get_barrier_semaphore()

    def greet(along, across):
        pl.semaphore_signal(barrier, inc=1, device_id=other(along, across), device_id_type=MESH)

    each_other(greet)

    node = iota((1, width), 1) % NP
    element = iota((1, width), 1) // NP
    row = iota((FACES * nz, width), 0)
    spreads = []
    covers = []
    for axis in range(AXES):
        fixed = axis_coords(node, axis)[0]
        covered = (fixed == 0) | (fixed == Q - 1)
        covers.append(covered)
        wanted = element * FACES + 2 * axis + jnp.where(fixed == 0, 0, 1)
        spreads.append(jnp.where(covered & (row == wanted), 1.0, 0.0).astype(jnp.float32))
    spread = jnp.concatenate(spreads, axis=1)
    aux[...] = jnp.zeros_like(aux)
    basis[...] = jnp.zeros_like(basis)

    for load in small:
        load.wait()
    for e in range(nz):
        for v in range(NV):
            basis[0, v : v + 1, e * NP : (e + 1) * NP] = (
                rhs[0, 0, e : e + 1, v * NP : (v + 1) * NP] * DOWN
            )
    for e in range(nz):
        for v in range(NV):
            aux[v * 8 : v * 8 + NV, e * FACES : (e + 1) * FACES] = face[:, v, e, :]
    line = iota((NV * 8, width), 0)
    same = jnp.where(line // 8 == line % 8, 1.0, 0.0).astype(jnp.float32)
    step_row = jnp.zeros((1, width), jnp.float32)
    for e in range(nz):
        step_row = jnp.where(element == e, inv_step[0, 0, e], step_row)
    own_part = same * step_row
    expanded = jnp.dot(
        aux[...], spread, precision=lax.Precision.HIGHEST, preferred_element_type=jnp.float32
    )
    for axis in range(AXES):
        at = slice(axis * width, (axis + 1) * width)
        half = 0.5 * expanded[:, at]
        jump = jnp.where(covers[axis], 0.5 * PENALTY * same, 0.0)
        wts[:, at] = half - jump
        own_part = own_part + (half + jump)
        fixed, first, second = axis_coords(node, axis)
        code = jnp.zeros((1, width), jnp.int32)
        for e in range(nz):
            side = jnp.where(fixed == 0, orient[0, 0, e, 2 * axis], orient[0, 0, e, 2 * axis + 1])
            code = jnp.where(element == e, side, code)
        swap, flip_first, flip_second = (code // 4) % 2, code % 2, (code // 2) % 2
        one = first + swap * (second - first)
        two = second + swap * (first - second)
        one = one + flip_first * (Q - 1 - 2 * one)
        two = two + flip_second * (Q - 1 - 2 * two)
        there = jnp.where(covers[axis], node_of(axis, Q - 1 - fixed, one, two), node)
        there = there + (element % 2) * NP
        turn[:, at] = jnp.broadcast_to(there, (8, width))
    own[...] = own_part

    for e in range(nz):
        loads[e].wait()
        start = e % 2 * NP
        for v in range(NV):
            mat[e // 2, v, :, start : start + NP] = held_vol[e, :, v * NP : (v + 1) * NP]

    sub = iota((8, lanes), 0)
    low = iota((NP, lanes), 1) < NP
    eye = iota((NP, lanes), 1) % NP == iota((NP, lanes), 0)

    def stack(parts):
        total = jnp.zeros((8, lanes), jnp.float32)
        for v in range(NV):
            total = jnp.where(sub == v, parts[v], total)
        return total

    for p in range(pairs):
        at = slice(p * lanes, (p + 1) * lanes)
        diagonal = stack(
            [
                jnp.sum(
                    jnp.where(eye, mat[p, v, v * NP : (v + 1) * NP, :], 0.0), axis=0, keepdims=True
                )
                for v in range(NV)
            ]
        )
        for v in range(NV):
            diagonal = diagonal + jnp.where(sub == v, own[v * 8 : v * 8 + 8, at], 0.0)
        dinv[:, at] = jnp.where(sub < NV, 1.0 / jnp.where(sub < NV, diagonal, 1.0), 0.0)

    def dense_product(blocks, value, p):
        at = slice(p * lanes, (p + 1) * lanes)
        parts = []
        for v in range(NV):
            total = blocks[p, 0, v * NP : (v + 1) * NP, :] * value[0:1, at]
            for w in range(1, NV):
                total = total + blocks[p, w, v * NP : (v + 1) * NP, :] * value[w : w + 1, at]
            left = jnp.sum(jnp.where(low, total, 0.0), axis=1, keepdims=True)
            right = jnp.sum(jnp.where(low, 0.0, total), axis=1, keepdims=True)
            placed = jnp.where(eye, jnp.where(low, left, right), 0.0)
            parts.append(jnp.sum(placed, axis=0, keepdims=True))
        return stack(parts)

    def series_product(blocks, value):
        return jnp.concatenate([dense_product(blocks, value, p) for p in range(pairs)], axis=1)

    def block_product(value):
        pieces = []
        for p in range(pairs):
            at = slice(p * lanes, (p + 1) * lanes)
            total = dense_product(mat, value, p)
            for w in range(NV):
                total = total + own[w * 8 : w * 8 + 8, at] * value[w : w + 1, at]
            pieces.append(total)
        return jnp.concatenate(pieces, axis=1)

    def face_product(axis, before, after):
        fixed = axis_coords(iota((8, width), 1) % NP, axis)[0]
        joined = jnp.where(fixed == Q - 1, before, after)
        pieces = []
        for p in range(pairs):
            at = slice(p * lanes, (p + 1) * lanes)
            here = slice(axis * width + p * lanes, axis * width + (p + 1) * lanes)
            turned = jnp.take_along_axis(
                joined[:, at], turn[:, here], axis=1, mode="promise_in_bounds"
            )
            total = wts[0:8, here] * turned[0:1, :]
            for w in range(1, NV):
                total = total + wts[w * 8 : w * 8 + 8, here] * turned[w : w + 1, :]
            pieces.append(total)
        return jnp.concatenate(pieces, axis=1)

    def put_right(p, v, w, tile):
        cut = slice(w * lanes, (w + 1) * lanes)
        upper, lower = slice(v * lanes, v * lanes + NP), slice(v * lanes + NP, (v + 1) * lanes)
        right_op[p, upper, cut] = jnp.where(low, tile, 0.0).astype(jnp.bfloat16)
        right_op[p, lower, cut] = jnp.where(low, 0.0, tile).astype(jnp.bfloat16)

    def first_powers():
        for p in range(pairs):
            for w in range(NV):
                at = slice(p * lanes, (p + 1) * lanes)
                for v in range(NV):
                    rows = slice(v * NP, (v + 1) * NP)
                    tile = mat[p, w, rows, :]
                    if v == w:
                        tile = jnp.where(eye, 0.0, tile)
                    else:
                        tile = tile + jnp.where(eye, own[w * 8 + v : w * 8 + v + 1, at], 0.0)
                    tile = -tile * dinv[w : w + 1, at]
                    series[p, w, rows, :] = tile
                    left_op[p, rows, w * lanes : (w + 1) * lanes] = tile.astype(jnp.bfloat16)
                    put_right(p, v, w, tile)
        for p in range(pairs):
            square = jnp.dot(left_op[p, 0:BLK, :], right_op[p], preferred_element_type=jnp.float32)
            for w in range(NV):
                cut = slice(w * lanes, (w + 1) * lanes)
                series[p, w] = series[p, w] + square[:, cut]
                left_op[p, BLK : 2 * BLK, cut] = square[:, cut].astype(jnp.bfloat16)
                for v in range(NV):
                    put_right(p, v, w, square[v * NP : (v + 1) * NP, cut])
        for p in range(pairs):
            both = jnp.dot(left_op[p], right_op[p], preferred_element_type=jnp.float32)
            for w in range(NV):
                cut = slice(w * lanes, (w + 1) * lanes)
                series[p, w] = series[p, w] + both[0:BLK, cut]
                fourth[p, w] = both[BLK : 2 * BLK, cut]

    def all_powers():
        for p in range(pairs):
            for w in range(NV):
                cut = slice(w * lanes, (w + 1) * lanes)
                left_op[p, 0:BLK, cut] = fourth[p, w].astype(jnp.bfloat16)
                for v in range(NV):
                    put_right(p, v, w, series[p, w, v * NP : (v + 1) * NP, :])
        for p in range(pairs):
            last = jnp.dot(left_op[p, 0:BLK, :], right_op[p], preferred_element_type=jnp.float32)
            for w in range(NV):
                cut = slice(w * lanes, (w + 1) * lanes)
                series[p, w] = series[p, w] + (fourth[p, w] + last[:, cut])

    def sum_copy(device):
        return pltpu.make_async_remote_copy(
            src_ref=packed.at[me],
            dst_ref=packed.at[me],
            send_sem=sum_send,
            recv_sem=sum_recv,
            device_id=device,
            device_id_type=MESH,
        )

    def dot(a, b):
        return jnp.sum(jnp.sum(a * b, axis=0, keepdims=True), axis=1, keepdims=True)

    def halo_copy(step, side):
        targets = [
            (lax.rem(gx + 1, nx), gy),
            (lax.rem(gx + nx - 1, nx), gy),
            (gx, lax.rem(gy + 1, ny)),
            (gx, lax.rem(gy + ny - 1, ny)),
        ]
        return pltpu.make_async_remote_copy(
            src_ref=dirs.at[step],
            dst_ref=halo.at[step, side],
            send_sem=halo_send.at[step, side],
            recv_sem=halo_recv.at[step, side],
            device_id=targets[side],
            device_id_type=MESH,
        )

    def apply_jacobian(step, meanwhile):
        for side in range(sides):
            halo_copy(step, side).start()
        direction = dirs[step]
        inner_part = block_product(direction) - basis[step]
        before, after = pltpu.roll(direction, NP, 1), pltpu.roll(direction, width - NP, 1)
        inner_part = inner_part + face_product(2, before, after)
        meanwhile()
        for side in range(sides):
            halo_copy(step, side).wait()
        basis[step + 1] = (
            inner_part
            + face_product(0, halo[step, 0], halo[step, 1])
            + face_product(1, halo[step, 2], halo[step, sides - 1])
        )

    state[...] = dinv[...] * basis[0]

    def sweep(_, inner):
        value = state[...]
        state[...] = value + dinv[...] * (basis[0] - block_product(value))
        return inner

    lax.fori_loop(0, SWEEPS, sweep, 0)
    dirs[0] = state[...]
    pl.semaphore_wait(barrier, devices - 1)
    apply_jacobian(0, first_powers)

    vector = basis[1]
    vector = vector + series_product(series, vector)
    dirs[1] = dinv[...] * (vector + series_product(fourth, vector))
    apply_jacobian(1, all_powers)

    vector = basis[2]
    dirs[2] = dinv[...] * (vector + series_product(series, vector))

    count = ITERS + 1
    where = iota((1, lanes), 1)
    zeros = jnp.zeros((1, lanes), jnp.float32)
    slots = {}
    for j in range(count):
        for i in range(j + 1):
            slots[i, j] = len(slots)
    peaks = []
    scaled = []
    rows = [zeros, zeros, zeros]

    def add_products(j):
        vector = basis[j]
        peak = jnp.max(jnp.max(jnp.abs(vector), axis=0, keepdims=True), axis=1, keepdims=True)
        peaks.append(peak)
        scaled.append(vector * jnp.where(peak > TINY, 1.0 / jnp.maximum(peak, TINY), 0.0))
        for i in range(j + 1):
            chosen = where == slots[i, j]
            for at, entry in enumerate([dot(scaled[i], scaled[j]), peaks[i], peaks[j]]):
                rows[at] = jnp.where(chosen, entry, rows[at])

    apply_jacobian(ITERS - 1, lambda: [add_products(j) for j in range(ITERS)])
    add_products(ITERS)
    row, row_peak, column_peak = rows
    packed[me, :, 0:lanes] = row
    packed[me, :, lanes : 2 * lanes] = row_peak
    packed[me, :, 2 * lanes : 3 * lanes] = column_peak

    each_other(lambda along, across: sum_copy(other(along, across)).start())
    arrived = packed.at[pl.ds(0, devices - 1)]
    pltpu.make_async_copy(arrived, arrived, sum_recv).wait()
    pltpu.make_async_copy(arrived, arrived, sum_send).wait()
    row_peaks = packed[:, :, lanes : 2 * lanes]
    column_peaks = packed[:, :, 2 * lanes : 3 * lanes]
    row_peak = jnp.max(row_peaks, axis=0)
    column_peak = jnp.max(column_peaks, axis=0)
    shares = (row_peaks * (1.0 / jnp.maximum(row_peak, TINY))) * (
        column_peaks * (1.0 / jnp.maximum(column_peak, TINY))
    )
    row = jnp.sum(packed[:, :, 0:lanes] * shares, axis=0)
    gram = {key: row[:, at : at + 1] for key, at in slots.items()}
    sizes = [row_peak[:, slots[i, i] : slots[i, i] + 1] for i in range(count)]
    upper = {}
    for i in range(count):
        for j in range(i, count):
            left = gram[i, j]
            for k in range(i):
                left = left - upper[k, i] * upper[k, j]
            upper[i, j] = jnp.sqrt(jnp.maximum(left, 0.0)) if i == j else left / upper[i, i]
    grown = [sizes[j + 1] / sizes[j] for j in range(ITERS)]
    zero = jnp.zeros((1, 1), jnp.float32)

    target = [upper[0, 0]] + [zero] * ITERS
    rotations = []
    columns = []
    for j in range(ITERS):
        column = [
            upper.get((i, j), zero) + grown[j] * upper[i, j + 1] for i in range(j + 2)
        ]
        for i in range(j):
            cosine, sine = rotations[i]
            column[i], column[i + 1] = (
                cosine * column[i] + sine * column[i + 1],
                cosine * column[i + 1] - sine * column[i],
            )
        radius = jnp.sqrt(column[j] * column[j] + column[j + 1] * column[j + 1])
        cosine, sine = column[j] / radius, column[j + 1] / radius
        rotations.append((cosine, sine))
        column[j] = radius
        target[j + 1] = -sine * target[j]
        target[j] = cosine * target[j]
        columns.append(column)
    solved = [None] * ITERS
    for i in reversed(range(ITERS)):
        left = target[i]
        for j in range(i + 1, ITERS):
            left = left - columns[j][i] * solved[j]
        solved[i] = left / columns[i][i]
    ratio[...] = jnp.abs(target[ITERS]) / upper[0, 0]
    update = solved[0] * (dirs[0] * (1.0 / DOWN))
    for j in range(1, ITERS):
        update = update + solved[j] * (dirs[j] * (sizes[0] / DOWN / sizes[j]))
    for e in range(nz):
        for v in range(NV):
            out[0, 0, e : e + 1, v * NP : (v + 1) * NP] = update[
                v : v + 1, e * NP : (e + 1) * NP
            ]


def solution(mesh):
    nx, ny = mesh.shape["gx"], mesh.shape["gy"]

    def body(rhs, vol_jac, inv_step, face_jac, orientation):
        nz = rhs.shape[2]
        width = nz * NP
        face = jnp.transpose(face_jac[0, 0], (2, 3, 0, 1))
        f32 = jnp.float32
        vmem = pl.BlockSpec(memory_space=pltpu.VMEM)
        dma = pltpu.SemaphoreType.DMA
        update, ratio = pl.pallas_call(
            lambda *refs: kernel(nx, ny, nz, *refs),
            out_shape=(
                jax.ShapeDtypeStruct(rhs.shape, f32),
                jax.ShapeDtypeStruct((1, 1), f32),
            ),
            in_specs=[pl.BlockSpec(memory_space=pl.ANY)] * 5,
            out_specs=(vmem, vmem),
            scratch_shapes=[
                pltpu.VMEM((nz, NV * NP, NV * NP), f32),
                pltpu.VMEM(rhs.shape, f32),
                pltpu.VMEM(face.shape, f32),
                pltpu.SMEM(inv_step.shape, f32),
                pltpu.SMEM(orientation.shape, jnp.int32),
                pltpu.VMEM((nz // 2, NV, NV * NP, 2 * NP), f32),
                pltpu.VMEM((NV * 8, FACES * nz), f32),
                pltpu.VMEM((NV * 8, AXES * width), f32),
                pltpu.VMEM((NV * 8, width), f32),
                pltpu.VMEM((8, AXES * width), jnp.int32),
                pltpu.VMEM((8, width), f32),
                pltpu.VMEM((ITERS + 1, 8, width), f32),
                pltpu.VMEM((ITERS, 8, width), f32),
                pltpu.VMEM((8, width), f32),
                pltpu.VMEM((ITERS, 4, 8, width), f32),
                pltpu.VMEM((nx * ny, 1, 6 * NP), f32),
                pltpu.VMEM((nz // 2, NV, NV * NP, 2 * NP), f32),
                pltpu.VMEM((nz // 2, NV, NV * NP, 2 * NP), f32),
                pltpu.VMEM((nz // 2, 2 * BLK, 2 * BLK), jnp.bfloat16),
                pltpu.VMEM((nz // 2, 2 * BLK, 2 * BLK), jnp.bfloat16),
                dma((nz,)),
                dma((4,)),
                dma((ITERS, 4)),
                dma((ITERS, 4)),
                dma,
                dma,
            ],
            compiler_params=pltpu.CompilerParams(collective_id=0, has_side_effects=True),
            name="newton_step",
        )(vol_jac, rhs, face, inv_step, orientation)
        return update, ratio[0, 0]

    placed = (
        P("gx", "gy", None, None),
        P("gx", "gy", None, None, None),
        P("gx", "gy", None),
        P("gx", "gy", None, None, None, None),
        P("gx", "gy", None, None),
    )
    return jax.shard_map(
        body,
        mesh=mesh,
        in_specs=placed,
        out_specs=(P("gx", "gy", None, None), P()),
        check_vma=False,
    )
```

```python
import jax
import jax.numpy as jnp
from jax import lax
from jax.experimental import pallas as pl
from jax.experimental.pallas import tpu as pltpu
from jax.sharding import PartitionSpec as P

Q = 4
NV = 5
ITERS = 3
NS_STEPS = 3
NP = Q**3
BLK = NV * NP
FACES = 6
AXES = 3
PENALTY = 4.0
MESH = pl.DeviceIdType.MESH
DOWN = 2.0**-40
TINY = 1e-36
UNROLL = 64


def iota(shape, dim):
    return lax.broadcasted_iota(jnp.int32, shape, dim)


def axis_coords(node, axis):
    first, second, third = node % Q, node // Q % Q, node // (Q * Q)
    pair = [(second, third), (first, third), (first, second)][axis]
    return [first, second, third][axis], pair[0], pair[1]


def node_of(axis, fixed, one, two):
    first, second, third = [(fixed, one, two), (one, fixed, two), (one, two, fixed)][axis]
    return first + Q * second + Q * Q * third


def kernel(
    nx, ny, nz,
    vol, rhs_in, face_in, step_in, orient_in,
    out, ratio,
    held_vol, rhs, face, inv_step, orient, factor, aux, wts, own, turn, dinv, basis, dirs, halo, packed,
    square, series, fourth, left_op, right_op, right_two,
    vol_sem, small_sem, halo_send, halo_recv, sum_send, sum_recv,
):
    gx, gy = lax.axis_index("gx"), lax.axis_index("gy")
    devices = nx * ny
    width = nz * NP
    pairs = nz // 2
    sides = 3 if ny == 2 else 4
    lanes = 2 * NP
    me = gx * ny + gy
    loads = [
        pltpu.make_async_copy(vol.at[0, 0, e], held_vol.at[e], vol_sem.at[e]) for e in range(nz)
    ]
    small = [
        pltpu.make_async_copy(source, target, small_sem.at[at])
        for at, (source, target) in enumerate(
            [(face_in, face), (orient_in, orient), (step_in, inv_step), (rhs_in, rhs)]
        )
    ]
    for load in small:
        load.start()
    for load in loads:
        load.start()

    def other(along, across):
        return lax.rem(gx + along, nx), lax.rem(gy + across, ny)

    def each_other(visit):
        if devices <= UNROLL:
            for step in range(1, devices):
                visit(step // ny, step % ny)
        else:
            def several(step, carry):
                visit(step // ny, step % ny)
                return carry

            lax.fori_loop(1, devices, several, 0)

    barrier = pltpu.get_barrier_semaphore()

    def greet(along, across):
        pl.semaphore_signal(barrier, inc=1, device_id=other(along, across), device_id_type=MESH)

    each_other(greet)

    node = iota((1, width), 1) % NP
    element = iota((1, width), 1) // NP
    row = iota((FACES * nz, width), 0)
    spreads = []
    covers = []
    for axis in range(AXES):
        fixed = axis_coords(node, axis)[0]
        covered = (fixed == 0) | (fixed == Q - 1)
        covers.append(covered)
        wanted = element * FACES + 2 * axis + jnp.where(fixed == 0, 0, 1)
        spreads.append(jnp.where(covered & (row == wanted), 1.0, 0.0).astype(jnp.float32))
    spread = jnp.concatenate(spreads, axis=1)
    aux[...] = jnp.zeros_like(aux)
    basis[...] = jnp.zeros_like(basis)

    for load in small:
        load.wait()
    for e in range(nz):
        for v in range(NV):
            basis[0, v : v + 1, e * NP : (e + 1) * NP] = (
                rhs[0, 0, e : e + 1, v * NP : (v + 1) * NP] * DOWN
            )
    for e in range(nz):
        for v in range(NV):
            aux[v * 8 : v * 8 + NV, e * FACES : (e + 1) * FACES] = face[:, v, e, :]
    line = iota((NV * 8, width), 0)
    same = jnp.where(line // 8 == line % 8, 1.0, 0.0).astype(jnp.float32)
    step_row = jnp.zeros((1, width), jnp.float32)
    for e in range(nz):
        step_row = jnp.where(element == e, inv_step[0, 0, e], step_row)
    own_part = same * step_row
    expanded = jnp.dot(
        aux[...], spread, precision=lax.Precision.HIGHEST, preferred_element_type=jnp.float32
    )
    for axis in range(AXES):
        at = slice(axis * width, (axis + 1) * width)
        half = 0.5 * expanded[:, at]
        jump = jnp.where(covers[axis], 0.5 * PENALTY * same, 0.0)
        wts[:, at] = half - jump
        own_part = own_part + (half + jump)
        fixed, first, second = axis_coords(node, axis)
        code = jnp.zeros((1, width), jnp.int32)
        for e in range(nz):
            side = jnp.where(fixed == 0, orient[0, 0, e, 2 * axis], orient[0, 0, e, 2 * axis + 1])
            code = jnp.where(element == e, side, code)
        swap, flip_first, flip_second = (code // 4) % 2, code % 2, (code // 2) % 2
        one = first + swap * (second - first)
        two = second + swap * (first - second)
        one = one + flip_first * (Q - 1 - 2 * one)
        two = two + flip_second * (Q - 1 - 2 * two)
        there = jnp.where(covers[axis], node_of(axis, Q - 1 - fixed, one, two), node)
        there = there + (element % 2) * NP
        turn[:, at] = jnp.broadcast_to(there, (8, width))
    own[...] = own_part

    sub = iota((8, lanes), 0)
    low = iota((NP, lanes), 1) < NP
    eye = iota((NP, lanes), 1) % NP == iota((NP, lanes), 0)

    def stack(parts):
        total = jnp.zeros((8, lanes), jnp.float32)
        for v in range(NV):
            total = jnp.where(sub == v, parts[v], total)
        return total

    dinv[...] = jnp.zeros_like(dinv)
    for p in range(pairs):
        at = slice(p * lanes, (p + 1) * lanes)
        loads[2 * p].wait()
        loads[2 * p + 1].wait()
        for w in range(NV):
            cut = slice(w * NP, (w + 1) * NP)

            def tile_of(v):
                rows = slice(v * NP, (v + 1) * NP)
                return jnp.concatenate(
                    [held_vol[2 * p, rows, cut], held_vol[2 * p + 1, rows, cut]], axis=1
                )

            middle = tile_of(w)
            diagonal = jnp.sum(jnp.where(eye, middle, 0.0), axis=0, keepdims=True)
            inverse = 1.0 / (diagonal + own[w * 9 : w * 9 + 1, at])
            dinv[w : w + 1, at] = inverse
            for v in range(NV):
                if v == w:
                    tile = jnp.where(eye, 0.0, middle)
                else:
                    tile = tile_of(v) + jnp.where(eye, own[w * 8 + v : w * 8 + v + 1, at], 0.0)
                factor[p, w, v * NP : (v + 1) * NP, :] = -tile * inverse

    def dense_product(blocks, value, p):
        at = slice(p * lanes, (p + 1) * lanes)
        parts = []
        for v in range(NV):
            total = blocks[p, 0, v * NP : (v + 1) * NP, :] * value[0:1, at]
            for w in range(1, NV):
                total = total + blocks[p, w, v * NP : (v + 1) * NP, :] * value[w : w + 1, at]
            left = jnp.sum(jnp.where(low, total, 0.0), axis=1, keepdims=True)
            right = jnp.sum(jnp.where(low, 0.0, total), axis=1, keepdims=True)
            placed = jnp.where(eye, jnp.where(low, left, right), 0.0)
            parts.append(jnp.sum(placed, axis=0, keepdims=True))
        return stack(parts)

    def power_product(blocks, value):
        return jnp.concatenate([dense_product(blocks, value, p) for p in range(pairs)], axis=1)

    def face_product(axis, before, after):
        fixed = axis_coords(iota((8, width), 1) % NP, axis)[0]
        joined = jnp.where(fixed == Q - 1, before, after)
        pieces = []
        for p in range(pairs):
            at = slice(p * lanes, (p + 1) * lanes)
            here = slice(axis * width + p * lanes, axis * width + (p + 1) * lanes)
            turned = jnp.take_along_axis(
                joined[:, at], turn[:, here], axis=1, mode="promise_in_bounds"
            )
            total = wts[0:8, here] * turned[0:1, :]
            for w in range(1, NV):
                total = total + wts[w * 8 : w * 8 + 8, here] * turned[w : w + 1, :]
            pieces.append(total)
        return jnp.concatenate(pieces, axis=1)

    def put_right(p, v, w, tile, target):
        cut = slice(w * lanes, (w + 1) * lanes)
        upper, lower = slice(v * lanes, v * lanes + NP), slice(v * lanes + NP, (v + 1) * lanes)
        target[p, upper, cut] = jnp.where(low, tile, 0.0).astype(jnp.bfloat16)
        target[p, lower, cut] = jnp.where(low, 0.0, tile).astype(jnp.bfloat16)

    def operands(p):
        for w in range(NV):
            for v in range(NV):
                rows = slice(v * NP, (v + 1) * NP)
                tile = factor[p, w, rows, :]
                left_op[p, rows, w * lanes : (w + 1) * lanes] = tile.astype(jnp.bfloat16)
                put_right(p, v, w, tile, right_op)

    def square_of(p):
        product = jnp.dot(left_op[p, 0:BLK, :], right_op[p], preferred_element_type=jnp.float32)
        for w in range(NV):
            square[p, w] = product[:, w * lanes : (w + 1) * lanes]

    def more_powers():
        for p in range(pairs):
            for w in range(NV):
                for v in range(NV):
                    rows = slice(v * NP, (v + 1) * NP)
                    tile = square[p, w, rows, :]
                    left_op[p, BLK + v * NP : BLK + (v + 1) * NP, w * lanes : (w + 1) * lanes] = (
                        tile.astype(jnp.bfloat16)
                    )
                    put_right(p, v, w, tile, right_two)
        for p in range(pairs):
            both = jnp.dot(left_op[p], right_two[p], preferred_element_type=jnp.float32)
            for w in range(NV):
                cut = slice(w * lanes, (w + 1) * lanes)
                series[p, w] = factor[p, w] + square[p, w] + both[0:BLK, cut]
                fourth[p, w] = both[BLK : 2 * BLK, cut]

    def all_powers():
        for p in range(pairs):
            for w in range(NV):
                cut = slice(w * lanes, (w + 1) * lanes)
                left_op[p, 0:BLK, cut] = fourth[p, w].astype(jnp.bfloat16)
                for v in range(NV):
                    put_right(p, v, w, series[p, w, v * NP : (v + 1) * NP, :], right_op)
        for p in range(pairs):
            last = jnp.dot(left_op[p, 0:BLK, :], right_op[p], preferred_element_type=jnp.float32)
            for w in range(NV):
                cut = slice(w * lanes, (w + 1) * lanes)
                series[p, w] = series[p, w] + (fourth[p, w] + last[:, cut])

    def sum_copy(device):
        return pltpu.make_async_remote_copy(
            src_ref=packed.at[me],
            dst_ref=packed.at[me],
            send_sem=sum_send,
            recv_sem=sum_recv,
            device_id=device,
            device_id_type=MESH,
        )

    def dot(a, b):
        return jnp.sum(jnp.sum(a * b, axis=0, keepdims=True), axis=1, keepdims=True)

    def halo_copy(step, side):
        targets = [
            (lax.rem(gx + 1, nx), gy),
            (lax.rem(gx + nx - 1, nx), gy),
            (gx, lax.rem(gy + 1, ny)),
            (gx, lax.rem(gy + ny - 1, ny)),
        ]
        return pltpu.make_async_remote_copy(
            src_ref=dirs.at[step],
            dst_ref=halo.at[step, side],
            send_sem=halo_send.at[step, side],
            recv_sem=halo_recv.at[step, side],
            device_id=targets[side],
            device_id_type=MESH,
        )

    def apply_jacobian(step, solved, meanwhile):
        direction = dinv[...] * solved
        dirs[step] = direction
        for side in range(sides):
            halo_copy(step, side).start()
        inner_part = (solved - basis[step]) - power_product(factor, solved)
        before, after = pltpu.roll(direction, NP, 1), pltpu.roll(direction, width - NP, 1)
        inner_part = inner_part + face_product(2, before, after)
        meanwhile()
        for side in range(sides):
            halo_copy(step, side).wait()
        basis[step + 1] = (
            inner_part
            + face_product(0, halo[step, 0], halo[step, 1])
            + face_product(1, halo[step, 2], halo[step, sides - 1])
        )

    begun = basis[0]
    solved = begun
    for sweep in range(3):
        solved = begun + power_product(factor, solved)
        for p in range(pairs):
            if sweep == p % 2:
                operands(p)
            if sweep == p % 2 + 1:
                square_of(p)
    solved = solved + power_product(square, power_product(square, solved))
    pl.semaphore_wait(barrier, devices - 1)
    apply_jacobian(0, solved, more_powers)

    solved = basis[1]
    solved = solved + power_product(series, solved)
    solved = solved + power_product(fourth, solved)
    apply_jacobian(1, solved, all_powers)

    solved = basis[2]
    solved = solved + power_product(series, solved)

    count = ITERS + 1
    where = iota((1, lanes), 1)
    zeros = jnp.zeros((1, lanes), jnp.float32)
    slots = {}
    for j in range(count):
        for i in range(j + 1):
            slots[i, j] = len(slots)
    peaks = []
    scaled = []
    rows = [zeros, zeros, zeros]

    def add_products(j):
        vector = basis[j]
        peak = jnp.max(jnp.max(jnp.abs(vector), axis=0, keepdims=True), axis=1, keepdims=True)
        peaks.append(peak)
        scaled.append(vector * jnp.where(peak > TINY, 1.0 / jnp.maximum(peak, TINY), 0.0))
        for i in range(j + 1):
            chosen = where == slots[i, j]
            for at, entry in enumerate([dot(scaled[i], scaled[j]), peaks[i], peaks[j]]):
                rows[at] = jnp.where(chosen, entry, rows[at])

    apply_jacobian(ITERS - 1, solved, lambda: [add_products(j) for j in range(ITERS)])
    add_products(ITERS)
    row, row_peak, column_peak = rows
    packed[me, :, 0:lanes] = row
    packed[me, :, lanes : 2 * lanes] = row_peak
    packed[me, :, 2 * lanes : 3 * lanes] = column_peak

    each_other(lambda along, across: sum_copy(other(along, across)).start())
    arrived = packed.at[pl.ds(0, devices - 1)]
    pltpu.make_async_copy(arrived, arrived, sum_recv).wait()
    pltpu.make_async_copy(arrived, arrived, sum_send).wait()
    row_peaks = packed[:, :, lanes : 2 * lanes]
    column_peaks = packed[:, :, 2 * lanes : 3 * lanes]
    row_peak = jnp.max(row_peaks, axis=0)
    column_peak = jnp.max(column_peaks, axis=0)
    shares = (row_peaks * (1.0 / jnp.maximum(row_peak, TINY))) * (
        column_peaks * (1.0 / jnp.maximum(column_peak, TINY))
    )
    row = jnp.sum(packed[:, :, 0:lanes] * shares, axis=0)
    gram = {key: row[:, at : at + 1] for key, at in slots.items()}
    sizes = [row_peak[:, slots[i, i] : slots[i, i] + 1] for i in range(count)]
    upper = {}
    for i in range(count):
        for j in range(i, count):
            left = gram[i, j]
            for k in range(i):
                left = left - upper[k, i] * upper[k, j]
            upper[i, j] = jnp.sqrt(jnp.maximum(left, 0.0)) if i == j else left / upper[i, i]
    grown = [sizes[j + 1] / sizes[j] for j in range(ITERS)]
    zero = jnp.zeros((1, 1), jnp.float32)

    target = [upper[0, 0]] + [zero] * ITERS
    rotations = []
    columns = []
    for j in range(ITERS):
        column = [
            upper.get((i, j), zero) + grown[j] * upper[i, j + 1] for i in range(j + 2)
        ]
        for i in range(j):
            cosine, sine = rotations[i]
            column[i], column[i + 1] = (
                cosine * column[i] + sine * column[i + 1],
                cosine * column[i + 1] - sine * column[i],
            )
        radius = jnp.sqrt(column[j] * column[j] + column[j + 1] * column[j + 1])
        cosine, sine = column[j] / radius, column[j + 1] / radius
        rotations.append((cosine, sine))
        column[j] = radius
        target[j + 1] = -sine * target[j]
        target[j] = cosine * target[j]
        columns.append(column)
    solved = [None] * ITERS
    for i in reversed(range(ITERS)):
        left = target[i]
        for j in range(i + 1, ITERS):
            left = left - columns[j][i] * solved[j]
        solved[i] = left / columns[i][i]
    ratio[...] = jnp.abs(target[ITERS]) / upper[0, 0]
    update = solved[0] * (dirs[0] * (1.0 / DOWN))
    for j in range(1, ITERS):
        update = update + solved[j] * (dirs[j] * (sizes[0] / DOWN / sizes[j]))
    for e in range(nz):
        for v in range(NV):
            out[0, 0, e : e + 1, v * NP : (v + 1) * NP] = update[
                v : v + 1, e * NP : (e + 1) * NP
            ]


def solution(mesh):
    nx, ny = mesh.shape["gx"], mesh.shape["gy"]

    def body(rhs, vol_jac, inv_step, face_jac, orientation):
        nz = rhs.shape[2]
        width = nz * NP
        face = jnp.transpose(face_jac[0, 0], (2, 3, 0, 1))
        f32 = jnp.float32
        vmem = pl.BlockSpec(memory_space=pltpu.VMEM)
        dma = pltpu.SemaphoreType.DMA
        update, ratio = pl.pallas_call(
            lambda *refs: kernel(nx, ny, nz, *refs),
            out_shape=(
                jax.ShapeDtypeStruct(rhs.shape, f32),
                jax.ShapeDtypeStruct((1, 1), f32),
            ),
            in_specs=[pl.BlockSpec(memory_space=pl.ANY)] * 5,
            out_specs=(vmem, vmem),
            scratch_shapes=[
                pltpu.VMEM((nz, NV * NP, NV * NP), f32),
                pltpu.VMEM(rhs.shape, f32),
                pltpu.VMEM(face.shape, f32),
                pltpu.SMEM(inv_step.shape, f32),
                pltpu.SMEM(orientation.shape, jnp.int32),
                pltpu.VMEM((nz // 2, NV, NV * NP, 2 * NP), f32),
                pltpu.VMEM((NV * 8, FACES * nz), f32),
                pltpu.VMEM((NV * 8, AXES * width), f32),
                pltpu.VMEM((NV * 8, width), f32),
                pltpu.VMEM((8, AXES * width), jnp.int32),
                pltpu.VMEM((8, width), f32),
                pltpu.VMEM((ITERS + 1, 8, width), f32),
                pltpu.VMEM((ITERS, 8, width), f32),
                pltpu.VMEM((ITERS, 4, 8, width), f32),
                pltpu.VMEM((nx * ny, 1, 6 * NP), f32),
                pltpu.VMEM((nz // 2, NV, NV * NP, 2 * NP), f32),
                pltpu.VMEM((nz // 2, NV, NV * NP, 2 * NP), f32),
                pltpu.VMEM((nz // 2, NV, NV * NP, 2 * NP), f32),
                pltpu.VMEM((nz // 2, 2 * BLK, 2 * BLK), jnp.bfloat16),
                pltpu.VMEM((nz // 2, 2 * BLK, 2 * BLK), jnp.bfloat16),
                pltpu.VMEM((nz // 2, 2 * BLK, 2 * BLK), jnp.bfloat16),
                dma((nz,)),
                dma((4,)),
                dma((ITERS, 4)),
                dma((ITERS, 4)),
                dma,
                dma,
            ],
            compiler_params=pltpu.CompilerParams(collective_id=0, has_side_effects=True),
            name="newton_step",
        )(vol_jac, rhs, face, inv_step, orientation)
        return update, ratio[0, 0]

    placed = (
        P("gx", "gy", None, None),
        P("gx", "gy", None, None, None),
        P("gx", "gy", None),
        P("gx", "gy", None, None, None, None),
        P("gx", "gy", None, None),
    )
    return jax.shard_map(
        body,
        mesh=mesh,
        in_specs=placed,
        out_specs=(P("gx", "gy", None, None), P()),
        check_vma=False,
    )
```

```python
import jax
import jax.numpy as jnp
from jax import lax
from jax.experimental import pallas as pl
from jax.experimental.pallas import tpu as pltpu
from jax.sharding import PartitionSpec as P

Q = 4
NV = 5
ITERS = 3
NS_STEPS = 3
NP = Q**3
BLK = NV * NP
FACES = 6
AXES = 3
PENALTY = 4.0
MESH = pl.DeviceIdType.MESH
DOWN = 2.0**-40
TINY = 1e-36
UNROLL = 64
GRANT = 24 * 2**20


def iota(shape, dim):
    return lax.broadcasted_iota(jnp.int32, shape, dim)


def axis_coords(node, axis):
    first, second, third = node % Q, node // Q % Q, node // (Q * Q)
    pair = [(second, third), (first, third), (first, second)][axis]
    return [first, second, third][axis], pair[0], pair[1]


def node_of(axis, fixed, one, two):
    first, second, third = [(fixed, one, two), (one, fixed, two), (one, two, fixed)][axis]
    return first + Q * second + Q * Q * third


def kernel(
    nx, ny, nz,
    vol, rhs_in, face_in, step_in, orient_in,
    out, ratio,
    held_vol, rhs, face, inv_step, orient, factor, aux, wts, own, turn, dinv, basis, dirs, halo, packed,
    square, series, fourth, left_op, right_op, right_two,
    out_held, ratio_held,
    vol_sem, small_sem, halo_send, halo_recv, sum_send, sum_recv, out_sem,
):
    gx, gy = lax.axis_index("gx"), lax.axis_index("gy")
    devices = nx * ny
    width = nz * NP
    pairs = nz // 2
    sides = 3 if ny == 2 else 4
    lanes = 2 * NP
    me = gx * ny + gy
    loads = [
        pltpu.make_async_copy(vol.at[0, 0, e], held_vol.at[e], vol_sem.at[e]) for e in range(nz)
    ]
    small = [
        pltpu.make_async_copy(source, target, small_sem.at[at])
        for at, (source, target) in enumerate(
            [(face_in, face), (orient_in, orient), (step_in, inv_step), (rhs_in, rhs)]
        )
    ]
    for load in small:
        load.start()
    for load in loads:
        load.start()

    def other(along, across):
        return lax.rem(gx + along, nx), lax.rem(gy + across, ny)

    def each_other(visit):
        if devices <= UNROLL:
            for step in range(1, devices):
                visit(step // ny, step % ny)
        else:
            def several(step, carry):
                visit(step // ny, step % ny)
                return carry

            lax.fori_loop(1, devices, several, 0)

    barrier = pltpu.get_barrier_semaphore()

    def greet(along, across):
        pl.semaphore_signal(barrier, inc=1, device_id=other(along, across), device_id_type=MESH)

    each_other(greet)

    node = iota((1, width), 1) % NP
    element = iota((1, width), 1) // NP
    row = iota((FACES * nz, width), 0)
    spreads = []
    covers = []
    for axis in range(AXES):
        fixed = axis_coords(node, axis)[0]
        covered = (fixed == 0) | (fixed == Q - 1)
        covers.append(covered)
        wanted = element * FACES + 2 * axis + jnp.where(fixed == 0, 0, 1)
        spreads.append(jnp.where(covered & (row == wanted), 1.0, 0.0).astype(jnp.float32))
    spread = jnp.concatenate(spreads, axis=1)
    aux[...] = jnp.zeros_like(aux)
    basis[...] = jnp.zeros_like(basis)

    for load in small:
        load.wait()
    for e in range(nz):
        for v in range(NV):
            basis[0, v : v + 1, e * NP : (e + 1) * NP] = (
                rhs[0, 0, e : e + 1, v * NP : (v + 1) * NP] * DOWN
            )
    for e in range(nz):
        for v in range(NV):
            aux[v * 8 : v * 8 + NV, e * FACES : (e + 1) * FACES] = face[:, v, e, :]
    line = iota((NV * 8, width), 0)
    same = jnp.where(line // 8 == line % 8, 1.0, 0.0).astype(jnp.float32)
    step_row = jnp.zeros((1, width), jnp.float32)
    for e in range(nz):
        step_row = jnp.where(element == e, inv_step[0, 0, e], step_row)
    own_part = same * step_row
    expanded = jnp.dot(
        aux[...], spread, precision=lax.Precision.HIGHEST, preferred_element_type=jnp.float32
    )
    for axis in range(AXES):
        at = slice(axis * width, (axis + 1) * width)
        half = 0.5 * expanded[:, at]
        jump = jnp.where(covers[axis], 0.5 * PENALTY * same, 0.0)
        wts[:, at] = half - jump
        own_part = own_part + (half + jump)
        fixed, first, second = axis_coords(node, axis)
        code = jnp.zeros((1, width), jnp.int32)
        for e in range(nz):
            side = jnp.where(fixed == 0, orient[0, 0, e, 2 * axis], orient[0, 0, e, 2 * axis + 1])
            code = jnp.where(element == e, side, code)
        swap, flip_first, flip_second = (code // 4) % 2, code % 2, (code // 2) % 2
        one = first + swap * (second - first)
        two = second + swap * (first - second)
        one = one + flip_first * (Q - 1 - 2 * one)
        two = two + flip_second * (Q - 1 - 2 * two)
        there = jnp.where(covers[axis], node_of(axis, Q - 1 - fixed, one, two), node)
        there = there + (element % 2) * NP
        turn[:, at] = jnp.broadcast_to(there, (8, width))
    own[...] = own_part

    sub = iota((8, lanes), 0)
    low = iota((NP, lanes), 1) < NP
    eye = iota((NP, lanes), 1) % NP == iota((NP, lanes), 0)

    def stack(parts):
        total = jnp.zeros((8, lanes), jnp.float32)
        for v in range(NV):
            total = jnp.where(sub == v, parts[v], total)
        return total

    dinv[...] = jnp.zeros_like(dinv)
    for p in range(pairs):
        at = slice(p * lanes, (p + 1) * lanes)
        loads[2 * p].wait()
        loads[2 * p + 1].wait()
        for w in range(NV):
            cut = slice(w * NP, (w + 1) * NP)

            def tile_of(v):
                rows = slice(v * NP, (v + 1) * NP)
                return jnp.concatenate(
                    [held_vol[2 * p, rows, cut], held_vol[2 * p + 1, rows, cut]], axis=1
                )

            middle = tile_of(w)
            diagonal = jnp.sum(jnp.where(eye, middle, 0.0), axis=0, keepdims=True)
            inverse = 1.0 / (diagonal + own[w * 9 : w * 9 + 1, at])
            dinv[w : w + 1, at] = inverse
            for v in range(NV):
                if v == w:
                    tile = jnp.where(eye, 0.0, middle)
                else:
                    tile = tile_of(v) + jnp.where(eye, own[w * 8 + v : w * 8 + v + 1, at], 0.0)
                factor[p, w, v * NP : (v + 1) * NP, :] = -tile * inverse

    def dense_product(blocks, value, p):
        at = slice(p * lanes, (p + 1) * lanes)
        parts = []
        for v in range(NV):
            total = blocks[p, 0, v * NP : (v + 1) * NP, :] * value[0:1, at]
            for w in range(1, NV):
                total = total + blocks[p, w, v * NP : (v + 1) * NP, :] * value[w : w + 1, at]
            left = jnp.sum(jnp.where(low, total, 0.0), axis=1, keepdims=True)
            right = jnp.sum(jnp.where(low, 0.0, total), axis=1, keepdims=True)
            placed = jnp.where(eye, jnp.where(low, left, right), 0.0)
            parts.append(jnp.sum(placed, axis=0, keepdims=True))
        return stack(parts)

    def power_product(blocks, value):
        return jnp.concatenate([dense_product(blocks, value, p) for p in range(pairs)], axis=1)

    def face_product(axis, before, after):
        fixed = axis_coords(iota((8, width), 1) % NP, axis)[0]
        joined = jnp.where(fixed == Q - 1, before, after)
        pieces = []
        for p in range(pairs):
            at = slice(p * lanes, (p + 1) * lanes)
            here = slice(axis * width + p * lanes, axis * width + (p + 1) * lanes)
            turned = jnp.take_along_axis(
                joined[:, at], turn[:, here], axis=1, mode="promise_in_bounds"
            )
            total = wts[0:8, here] * turned[0:1, :]
            for w in range(1, NV):
                total = total + wts[w * 8 : w * 8 + 8, here] * turned[w : w + 1, :]
            pieces.append(total)
        return jnp.concatenate(pieces, axis=1)

    def put_right(p, v, w, tile, target):
        cut = slice(w * lanes, (w + 1) * lanes)
        upper, lower = slice(v * lanes, v * lanes + NP), slice(v * lanes + NP, (v + 1) * lanes)
        target[p, upper, cut] = jnp.where(low, tile, 0.0).astype(jnp.bfloat16)
        target[p, lower, cut] = jnp.where(low, 0.0, tile).astype(jnp.bfloat16)

    def operands(p):
        for w in range(NV):
            for v in range(NV):
                rows = slice(v * NP, (v + 1) * NP)
                tile = factor[p, w, rows, :]
                left_op[p, rows, w * lanes : (w + 1) * lanes] = tile.astype(jnp.bfloat16)
                put_right(p, v, w, tile, right_op)

    def square_of(p):
        product = jnp.dot(left_op[p, 0:BLK, :], right_op[p], preferred_element_type=jnp.float32)
        for w in range(NV):
            square[p, w] = product[:, w * lanes : (w + 1) * lanes]

    def more_powers():
        for p in range(pairs):
            for w in range(NV):
                for v in range(NV):
                    rows = slice(v * NP, (v + 1) * NP)
                    tile = square[p, w, rows, :]
                    left_op[p, BLK + v * NP : BLK + (v + 1) * NP, w * lanes : (w + 1) * lanes] = (
                        tile.astype(jnp.bfloat16)
                    )
                    put_right(p, v, w, tile, right_two)
        for p in range(pairs):
            both = jnp.dot(left_op[p], right_two[p], preferred_element_type=jnp.float32)
            for w in range(NV):
                cut = slice(w * lanes, (w + 1) * lanes)
                series[p, w] = factor[p, w] + square[p, w] + both[0:BLK, cut]
                fourth[p, w] = both[BLK : 2 * BLK, cut]

    def all_powers():
        for p in range(pairs):
            for w in range(NV):
                cut = slice(w * lanes, (w + 1) * lanes)
                left_op[p, 0:BLK, cut] = fourth[p, w].astype(jnp.bfloat16)
                for v in range(NV):
                    put_right(p, v, w, series[p, w, v * NP : (v + 1) * NP, :], right_op)
        for p in range(pairs):
            last = jnp.dot(left_op[p, 0:BLK, :], right_op[p], preferred_element_type=jnp.float32)
            for w in range(NV):
                cut = slice(w * lanes, (w + 1) * lanes)
                series[p, w] = series[p, w] + (fourth[p, w] + last[:, cut])

    def sum_copy(device):
        return pltpu.make_async_remote_copy(
            src_ref=packed.at[me],
            dst_ref=packed.at[me],
            send_sem=sum_send,
            recv_sem=sum_recv,
            device_id=device,
            device_id_type=MESH,
        )

    def dot(a, b):
        return jnp.sum(jnp.sum(a * b, axis=0, keepdims=True), axis=1, keepdims=True)

    def halo_copy(step, side):
        targets = [
            (lax.rem(gx + 1, nx), gy),
            (lax.rem(gx + nx - 1, nx), gy),
            (gx, lax.rem(gy + 1, ny)),
            (gx, lax.rem(gy + ny - 1, ny)),
        ]
        return pltpu.make_async_remote_copy(
            src_ref=dirs.at[step],
            dst_ref=halo.at[step, side],
            send_sem=halo_send.at[step, side],
            recv_sem=halo_recv.at[step, side],
            device_id=targets[side],
            device_id_type=MESH,
        )

    def apply_jacobian(step, solved, meanwhile):
        direction = dinv[...] * solved
        dirs[step] = direction
        for side in range(sides):
            halo_copy(step, side).start()
        inner_part = (solved - basis[step]) - power_product(factor, solved)
        before, after = pltpu.roll(direction, NP, 1), pltpu.roll(direction, width - NP, 1)
        inner_part = inner_part + face_product(2, before, after)
        meanwhile()
        for side in range(sides):
            halo_copy(step, side).wait()
        basis[step + 1] = (
            inner_part
            + face_product(0, halo[step, 0], halo[step, 1])
            + face_product(1, halo[step, 2], halo[step, sides - 1])
        )

    begun = basis[0]
    solved = begun
    for sweep in range(3):
        solved = begun + power_product(factor, solved)
        for p in range(pairs):
            if sweep == p % 2:
                operands(p)
            if sweep == p % 2 + 1:
                square_of(p)
    solved = solved + power_product(square, power_product(square, solved))
    pl.semaphore_wait(barrier, devices - 1)
    apply_jacobian(0, solved, more_powers)

    solved = basis[1]
    solved = solved + power_product(series, solved)
    solved = solved + power_product(fourth, solved)
    apply_jacobian(1, solved, all_powers)

    solved = basis[2]
    solved = solved + power_product(series, solved)

    count = ITERS + 1
    where = iota((1, lanes), 1)
    zeros = jnp.zeros((1, lanes), jnp.float32)
    slots = {}
    for j in range(count):
        for i in range(j + 1):
            slots[i, j] = len(slots)
    peaks = []
    scaled = []
    rows = [zeros, zeros, zeros]

    def add_products(j):
        vector = basis[j]
        peak = jnp.max(jnp.max(jnp.abs(vector), axis=0, keepdims=True), axis=1, keepdims=True)
        peaks.append(peak)
        scaled.append(vector * jnp.where(peak > TINY, 1.0 / jnp.maximum(peak, TINY), 0.0))
        for i in range(j + 1):
            chosen = where == slots[i, j]
            for at, entry in enumerate([dot(scaled[i], scaled[j]), peaks[i], peaks[j]]):
                rows[at] = jnp.where(chosen, entry, rows[at])

    apply_jacobian(ITERS - 1, solved, lambda: [add_products(j) for j in range(ITERS)])
    add_products(ITERS)
    row, row_peak, column_peak = rows
    packed[me, :, 0:lanes] = row
    packed[me, :, lanes : 2 * lanes] = row_peak
    packed[me, :, 2 * lanes : 3 * lanes] = column_peak

    each_other(lambda along, across: sum_copy(other(along, across)).start())
    arrived = packed.at[pl.ds(0, devices - 1)]
    pltpu.make_async_copy(arrived, arrived, sum_recv).wait()
    pltpu.make_async_copy(arrived, arrived, sum_send).wait()
    row_peaks = packed[:, :, lanes : 2 * lanes]
    column_peaks = packed[:, :, 2 * lanes : 3 * lanes]
    row_peak = jnp.max(row_peaks, axis=0)
    column_peak = jnp.max(column_peaks, axis=0)
    shares = (row_peaks * (1.0 / jnp.maximum(row_peak, TINY))) * (
        column_peaks * (1.0 / jnp.maximum(column_peak, TINY))
    )
    row = jnp.sum(packed[:, :, 0:lanes] * shares, axis=0)
    gram = {key: row[:, at : at + 1] for key, at in slots.items()}
    sizes = [row_peak[:, slots[i, i] : slots[i, i] + 1] for i in range(count)]
    upper = {}
    for i in range(count):
        for j in range(i, count):
            left = gram[i, j]
            for k in range(i):
                left = left - upper[k, i] * upper[k, j]
            upper[i, j] = jnp.sqrt(jnp.maximum(left, 0.0)) if i == j else left / upper[i, i]
    grown = [sizes[j + 1] / sizes[j] for j in range(ITERS)]
    zero = jnp.zeros((1, 1), jnp.float32)

    target = [upper[0, 0]] + [zero] * ITERS
    rotations = []
    columns = []
    for j in range(ITERS):
        column = [
            upper.get((i, j), zero) + grown[j] * upper[i, j + 1] for i in range(j + 2)
        ]
        for i in range(j):
            cosine, sine = rotations[i]
            column[i], column[i + 1] = (
                cosine * column[i] + sine * column[i + 1],
                cosine * column[i + 1] - sine * column[i],
            )
        radius = jnp.sqrt(column[j] * column[j] + column[j + 1] * column[j + 1])
        cosine, sine = column[j] / radius, column[j + 1] / radius
        rotations.append((cosine, sine))
        column[j] = radius
        target[j + 1] = -sine * target[j]
        target[j] = cosine * target[j]
        columns.append(column)
    solved = [None] * ITERS
    for i in reversed(range(ITERS)):
        left = target[i]
        for j in range(i + 1, ITERS):
            left = left - columns[j][i] * solved[j]
        solved[i] = left / columns[i][i]
    ratio_held[...] = jnp.abs(target[ITERS]) / upper[0, 0]
    update = solved[0] * (dirs[0] * (1.0 / DOWN))
    for j in range(1, ITERS):
        update = update + solved[j] * (dirs[j] * (sizes[0] / DOWN / sizes[j]))
    for e in range(nz):
        for v in range(NV):
            out_held[0, 0, e : e + 1, v * NP : (v + 1) * NP] = update[
                v : v + 1, e * NP : (e + 1) * NP
            ]
    stores = [
        pltpu.make_async_copy(out_held, out, out_sem.at[0]),
        pltpu.make_async_copy(ratio_held, ratio, out_sem.at[1]),
    ]
    for store in stores:
        store.start()
    for store in stores:
        store.wait()


def solution(mesh):
    nx, ny = mesh.shape["gx"], mesh.shape["gy"]

    def body(rhs, vol_jac, inv_step, face_jac, orientation):
        nz = rhs.shape[2]
        width = nz * NP
        face = jnp.transpose(face_jac[0, 0], (2, 3, 0, 1))
        f32 = jnp.float32
        vmem = pl.BlockSpec(memory_space=pltpu.VMEM)
        dma = pltpu.SemaphoreType.DMA
        update, ratio = pl.pallas_call(
            lambda *refs: kernel(nx, ny, nz, *refs),
            out_shape=(
                jax.ShapeDtypeStruct(rhs.shape, f32),
                jax.ShapeDtypeStruct((1, 1), f32),
            ),
            in_specs=[pl.BlockSpec(memory_space=pltpu.HBM)] * 5,
            out_specs=(pl.BlockSpec(memory_space=pl.ANY), pl.BlockSpec(memory_space=pl.ANY)),
            scratch_shapes=[
                pltpu.VMEM((nz, NV * NP, NV * NP), f32),
                pltpu.VMEM(rhs.shape, f32),
                pltpu.VMEM(face.shape, f32),
                pltpu.SMEM(inv_step.shape, f32),
                pltpu.SMEM(orientation.shape, jnp.int32),
                pltpu.VMEM((nz // 2, NV, NV * NP, 2 * NP), f32),
                pltpu.VMEM((NV * 8, FACES * nz), f32),
                pltpu.VMEM((NV * 8, AXES * width), f32),
                pltpu.VMEM((NV * 8, width), f32),
                pltpu.VMEM((8, AXES * width), jnp.int32),
                pltpu.VMEM((8, width), f32),
                pltpu.VMEM((ITERS + 1, 8, width), f32),
                pltpu.VMEM((ITERS, 8, width), f32),
                pltpu.VMEM((ITERS, 4, 8, width), f32),
                pltpu.VMEM((nx * ny, 1, 6 * NP), f32),
                pltpu.VMEM((nz // 2, NV, NV * NP, 2 * NP), f32),
                pltpu.VMEM((nz // 2, NV, NV * NP, 2 * NP), f32),
                pltpu.VMEM((nz // 2, NV, NV * NP, 2 * NP), f32),
                pltpu.VMEM((nz // 2, 2 * BLK, 2 * BLK), jnp.bfloat16),
                pltpu.VMEM((nz // 2, 2 * BLK, 2 * BLK), jnp.bfloat16),
                pltpu.VMEM((nz // 2, 2 * BLK, 2 * BLK), jnp.bfloat16),
                pltpu.VMEM(rhs.shape, f32),
                pltpu.VMEM((1, 1), f32),
                dma((nz,)),
                dma((4,)),
                dma((ITERS, 4)),
                dma((ITERS, 4)),
                dma,
                dma,
                dma((2,)),
            ],
            compiler_params=pltpu.CompilerParams(
                collective_id=0, has_side_effects=True, vmem_limit_bytes=GRANT
            ),
            name="newton_step",
        )(
            *[
                pltpu.with_memory_space_constraint(value, pltpu.HBM)
                for value in (vol_jac, rhs, face, inv_step, orientation)
            ]
        )
        return update, ratio[0, 0]

    placed = (
        P("gx", "gy", None, None),
        P("gx", "gy", None, None, None),
        P("gx", "gy", None),
        P("gx", "gy", None, None, None, None),
        P("gx", "gy", None, None),
    )
    return jax.shard_map(
        body,
        mesh=mesh,
        in_specs=placed,
        out_specs=(P("gx", "gy", None, None), P()),
        check_vma=False,
    )
```

```python
import jax
import jax.numpy as jnp
from jax import lax
from jax.experimental import pallas as pl
from jax.experimental.pallas import tpu as pltpu
from jax.sharding import PartitionSpec as P

Q = 4
NV = 5
ITERS = 3
NS_STEPS = 3
NP = Q**3
BLK = NV * NP
FACES = 6
AXES = 3
PENALTY = 4.0
MESH = pl.DeviceIdType.MESH
DOWN = 2.0**-40
TINY = 1e-36
UNROLL = 64
GRANT = 24 * 2**20


def iota(shape, dim):
    return lax.broadcasted_iota(jnp.int32, shape, dim)


def axis_coords(node, axis):
    first, second, third = node % Q, node // Q % Q, node // (Q * Q)
    pair = [(second, third), (first, third), (first, second)][axis]
    return [first, second, third][axis], pair[0], pair[1]


def node_of(axis, fixed, one, two):
    first, second, third = [(fixed, one, two), (one, fixed, two), (one, two, fixed)][axis]
    return first + Q * second + Q * Q * third


def kernel(
    nx, ny, nz,
    vol, rhs_in, face_in, step_in, orient_in,
    out,
    held_vol, rhs, face, inv_step, orient, factor, aux, wts, own, turn, dinv, basis, dirs, halo, packed,
    square, series, fourth, left_op, right_op, right_two,
    out_held,
    vol_sem, small_sem, halo_send, halo_recv, sum_send, sum_recv, out_sem,
):
    gx, gy = lax.axis_index("gx"), lax.axis_index("gy")
    devices = nx * ny
    width = nz * NP
    pairs = nz // 2
    sides = 3 if ny == 2 else 4
    lanes = 2 * NP
    me = gx * ny + gy
    loads = [
        pltpu.make_async_copy(vol.at[0, 0, e], held_vol.at[e], vol_sem.at[e]) for e in range(nz)
    ]
    small = [
        pltpu.make_async_copy(source, target, small_sem.at[at])
        for at, (source, target) in enumerate(
            [(face_in, face), (orient_in, orient), (step_in, inv_step), (rhs_in, rhs)]
        )
    ]
    for load in small:
        load.start()
    for load in loads:
        load.start()

    def other(along, across):
        return lax.rem(gx + along, nx), lax.rem(gy + across, ny)

    def each_other(visit):
        if devices <= UNROLL:
            for step in range(1, devices):
                visit(step // ny, step % ny)
        else:
            def several(step, carry):
                visit(step // ny, step % ny)
                return carry

            lax.fori_loop(1, devices, several, 0)

    barrier = pltpu.get_barrier_semaphore()

    def greet(along, across):
        pl.semaphore_signal(barrier, inc=1, device_id=other(along, across), device_id_type=MESH)

    each_other(greet)

    node = iota((1, width), 1) % NP
    element = iota((1, width), 1) // NP
    row = iota((FACES * nz, width), 0)
    spreads = []
    covers = []
    for axis in range(AXES):
        fixed = axis_coords(node, axis)[0]
        covered = (fixed == 0) | (fixed == Q - 1)
        covers.append(covered)
        wanted = element * FACES + 2 * axis + jnp.where(fixed == 0, 0, 1)
        spreads.append(jnp.where(covered & (row == wanted), 1.0, 0.0).astype(jnp.float32))
    spread = jnp.concatenate(spreads, axis=1)
    aux[...] = jnp.zeros_like(aux)
    basis[...] = jnp.zeros_like(basis)

    for load in small:
        load.wait()
    for e in range(nz):
        for v in range(NV):
            basis[0, v : v + 1, e * NP : (e + 1) * NP] = (
                rhs[0, 0, e : e + 1, v * NP : (v + 1) * NP] * DOWN
            )
    for e in range(nz):
        for v in range(NV):
            aux[v * 8 : v * 8 + NV, e * FACES : (e + 1) * FACES] = face[:, v, e, :]
    line = iota((NV * 8, width), 0)
    same = jnp.where(line // 8 == line % 8, 1.0, 0.0).astype(jnp.float32)
    step_row = jnp.zeros((1, width), jnp.float32)
    for e in range(nz):
        step_row = jnp.where(element == e, inv_step[0, 0, e], step_row)
    own_part = same * step_row
    expanded = jnp.dot(
        aux[...], spread, precision=lax.Precision.HIGHEST, preferred_element_type=jnp.float32
    )
    for axis in range(AXES):
        at = slice(axis * width, (axis + 1) * width)
        half = 0.5 * expanded[:, at]
        jump = jnp.where(covers[axis], 0.5 * PENALTY * same, 0.0)
        wts[:, at] = half - jump
        own_part = own_part + (half + jump)
        fixed, first, second = axis_coords(node, axis)
        code = jnp.zeros((1, width), jnp.int32)
        for e in range(nz):
            side = jnp.where(fixed == 0, orient[0, 0, e, 2 * axis], orient[0, 0, e, 2 * axis + 1])
            code = jnp.where(element == e, side, code)
        swap, flip_first, flip_second = (code // 4) % 2, code % 2, (code // 2) % 2
        one = first + swap * (second - first)
        two = second + swap * (first - second)
        one = one + flip_first * (Q - 1 - 2 * one)
        two = two + flip_second * (Q - 1 - 2 * two)
        there = jnp.where(covers[axis], node_of(axis, Q - 1 - fixed, one, two), node)
        there = there + (element % 2) * NP
        turn[:, at] = jnp.broadcast_to(there, (8, width))
    own[...] = own_part

    sub = iota((8, lanes), 0)
    low = iota((NP, lanes), 1) < NP
    eye = iota((NP, lanes), 1) % NP == iota((NP, lanes), 0)

    def stack(parts):
        total = jnp.zeros((8, lanes), jnp.float32)
        for v in range(NV):
            total = jnp.where(sub == v, parts[v], total)
        return total

    dinv[...] = jnp.zeros_like(dinv)
    for p in range(pairs):
        at = slice(p * lanes, (p + 1) * lanes)
        loads[2 * p].wait()
        loads[2 * p + 1].wait()
        for w in range(NV):
            cut = slice(w * NP, (w + 1) * NP)

            def tile_of(v):
                rows = slice(v * NP, (v + 1) * NP)
                return jnp.concatenate(
                    [held_vol[2 * p, rows, cut], held_vol[2 * p + 1, rows, cut]], axis=1
                )

            middle = tile_of(w)
            diagonal = jnp.sum(jnp.where(eye, middle, 0.0), axis=0, keepdims=True)
            inverse = 1.0 / (diagonal + own[w * 9 : w * 9 + 1, at])
            dinv[w : w + 1, at] = inverse
            for v in range(NV):
                if v == w:
                    tile = jnp.where(eye, 0.0, middle)
                else:
                    tile = tile_of(v) + jnp.where(eye, own[w * 8 + v : w * 8 + v + 1, at], 0.0)
                factor[p, w, v * NP : (v + 1) * NP, :] = -tile * inverse

    def dense_product(blocks, value, p):
        at = slice(p * lanes, (p + 1) * lanes)
        parts = []
        for v in range(NV):
            total = blocks[p, 0, v * NP : (v + 1) * NP, :] * value[0:1, at]
            for w in range(1, NV):
                total = total + blocks[p, w, v * NP : (v + 1) * NP, :] * value[w : w + 1, at]
            left = jnp.sum(jnp.where(low, total, 0.0), axis=1, keepdims=True)
            right = jnp.sum(jnp.where(low, 0.0, total), axis=1, keepdims=True)
            placed = jnp.where(eye, jnp.where(low, left, right), 0.0)
            parts.append(jnp.sum(placed, axis=0, keepdims=True))
        return stack(parts)

    def power_product(blocks, value):
        return jnp.concatenate([dense_product(blocks, value, p) for p in range(pairs)], axis=1)

    def face_product(axis, before, after):
        fixed = axis_coords(iota((8, width), 1) % NP, axis)[0]
        joined = jnp.where(fixed == Q - 1, before, after)
        pieces = []
        for p in range(pairs):
            at = slice(p * lanes, (p + 1) * lanes)
            here = slice(axis * width + p * lanes, axis * width + (p + 1) * lanes)
            turned = jnp.take_along_axis(
                joined[:, at], turn[:, here], axis=1, mode="promise_in_bounds"
            )
            total = wts[0:8, here] * turned[0:1, :]
            for w in range(1, NV):
                total = total + wts[w * 8 : w * 8 + 8, here] * turned[w : w + 1, :]
            pieces.append(total)
        return jnp.concatenate(pieces, axis=1)

    def put_right(p, v, w, tile, target):
        cut = slice(w * lanes, (w + 1) * lanes)
        upper, lower = slice(v * lanes, v * lanes + NP), slice(v * lanes + NP, (v + 1) * lanes)
        target[p, upper, cut] = jnp.where(low, tile, 0.0).astype(jnp.bfloat16)
        target[p, lower, cut] = jnp.where(low, 0.0, tile).astype(jnp.bfloat16)

    def operands(p):
        for w in range(NV):
            for v in range(NV):
                rows = slice(v * NP, (v + 1) * NP)
                tile = factor[p, w, rows, :]
                left_op[p, rows, w * lanes : (w + 1) * lanes] = tile.astype(jnp.bfloat16)
                put_right(p, v, w, tile, right_op)

    def square_of(p):
        product = jnp.dot(left_op[p, 0:BLK, :], right_op[p], preferred_element_type=jnp.float32)
        for w in range(NV):
            square[p, w] = product[:, w * lanes : (w + 1) * lanes]

    def more_powers():
        for p in range(pairs):
            for w in range(NV):
                for v in range(NV):
                    rows = slice(v * NP, (v + 1) * NP)
                    tile = square[p, w, rows, :]
                    left_op[p, BLK + v * NP : BLK + (v + 1) * NP, w * lanes : (w + 1) * lanes] = (
                        tile.astype(jnp.bfloat16)
                    )
                    put_right(p, v, w, tile, right_two)
        for p in range(pairs):
            both = jnp.dot(left_op[p], right_two[p], preferred_element_type=jnp.float32)
            for w in range(NV):
                cut = slice(w * lanes, (w + 1) * lanes)
                series[p, w] = factor[p, w] + square[p, w] + both[0:BLK, cut]
                fourth[p, w] = both[BLK : 2 * BLK, cut]

    def all_powers():
        for p in range(pairs):
            for w in range(NV):
                cut = slice(w * lanes, (w + 1) * lanes)
                left_op[p, 0:BLK, cut] = fourth[p, w].astype(jnp.bfloat16)
                for v in range(NV):
                    put_right(p, v, w, series[p, w, v * NP : (v + 1) * NP, :], right_op)
        for p in range(pairs):
            last = jnp.dot(left_op[p, 0:BLK, :], right_op[p], preferred_element_type=jnp.float32)
            for w in range(NV):
                cut = slice(w * lanes, (w + 1) * lanes)
                series[p, w] = series[p, w] + (fourth[p, w] + last[:, cut])

    def sum_copy(device):
        return pltpu.make_async_remote_copy(
            src_ref=packed.at[me],
            dst_ref=packed.at[me],
            send_sem=sum_send,
            recv_sem=sum_recv,
            device_id=device,
            device_id_type=MESH,
        )

    def dot(a, b):
        return jnp.sum(jnp.sum(a * b, axis=0, keepdims=True), axis=1, keepdims=True)

    def halo_copy(step, side):
        targets = [
            (lax.rem(gx + 1, nx), gy),
            (lax.rem(gx + nx - 1, nx), gy),
            (gx, lax.rem(gy + 1, ny)),
            (gx, lax.rem(gy + ny - 1, ny)),
        ]
        return pltpu.make_async_remote_copy(
            src_ref=dirs.at[step],
            dst_ref=halo.at[step, side],
            send_sem=halo_send.at[step, side],
            recv_sem=halo_recv.at[step, side],
            device_id=targets[side],
            device_id_type=MESH,
        )

    def apply_jacobian(step, solved, meanwhile):
        direction = dinv[...] * solved
        dirs[step] = direction
        for side in range(sides):
            halo_copy(step, side).start()
        inner_part = (solved - basis[step]) - power_product(factor, solved)
        before, after = pltpu.roll(direction, NP, 1), pltpu.roll(direction, width - NP, 1)
        inner_part = inner_part + face_product(2, before, after)
        meanwhile()
        for side in range(sides):
            halo_copy(step, side).wait()
        basis[step + 1] = (
            inner_part
            + face_product(0, halo[step, 0], halo[step, 1])
            + face_product(1, halo[step, 2], halo[step, sides - 1])
        )

    begun = basis[0]
    solved = begun
    for sweep in range(3):
        solved = begun + power_product(factor, solved)
        for p in range(pairs):
            if sweep == p % 2:
                operands(p)
            if sweep == p % 2 + 1:
                square_of(p)
    solved = solved + power_product(square, power_product(square, solved))
    pl.semaphore_wait(barrier, devices - 1)
    apply_jacobian(0, solved, more_powers)

    solved = basis[1]
    solved = solved + power_product(series, solved)
    solved = solved + power_product(fourth, solved)
    apply_jacobian(1, solved, all_powers)

    solved = basis[2]
    solved = solved + power_product(series, solved)

    count = ITERS + 1
    where = iota((1, lanes), 1)
    zeros = jnp.zeros((1, lanes), jnp.float32)
    slots = {}
    for j in range(count):
        for i in range(j + 1):
            slots[i, j] = len(slots)
    peaks = []
    scaled = []
    rows = [zeros, zeros, zeros]

    def add_products(j):
        vector = basis[j]
        peak = jnp.max(jnp.max(jnp.abs(vector), axis=0, keepdims=True), axis=1, keepdims=True)
        peaks.append(peak)
        scaled.append(vector * jnp.where(peak > TINY, 1.0 / jnp.maximum(peak, TINY), 0.0))
        for i in range(j + 1):
            chosen = where == slots[i, j]
            for at, entry in enumerate([dot(scaled[i], scaled[j]), peaks[i], peaks[j]]):
                rows[at] = jnp.where(chosen, entry, rows[at])

    apply_jacobian(ITERS - 1, solved, lambda: [add_products(j) for j in range(ITERS)])
    add_products(ITERS)
    row, row_peak, column_peak = rows
    packed[me, :, 0:lanes] = row
    packed[me, :, lanes : 2 * lanes] = row_peak
    packed[me, :, 2 * lanes : 3 * lanes] = column_peak

    each_other(lambda along, across: sum_copy(other(along, across)).start())
    arrived = packed.at[pl.ds(0, devices - 1)]
    pltpu.make_async_copy(arrived, arrived, sum_recv).wait()
    pltpu.make_async_copy(arrived, arrived, sum_send).wait()
    row_peaks = packed[:, :, lanes : 2 * lanes]
    column_peaks = packed[:, :, 2 * lanes : 3 * lanes]
    row_peak = jnp.max(row_peaks, axis=0)
    column_peak = jnp.max(column_peaks, axis=0)
    shares = (row_peaks * (1.0 / jnp.maximum(row_peak, TINY))) * (
        column_peaks * (1.0 / jnp.maximum(column_peak, TINY))
    )
    row = jnp.sum(packed[:, :, 0:lanes] * shares, axis=0)
    gram = {key: row[:, at : at + 1] for key, at in slots.items()}
    sizes = [row_peak[:, slots[i, i] : slots[i, i] + 1] for i in range(count)]
    upper = {}
    for i in range(count):
        for j in range(i, count):
            left = gram[i, j]
            for k in range(i):
                left = left - upper[k, i] * upper[k, j]
            upper[i, j] = jnp.sqrt(jnp.maximum(left, 0.0)) if i == j else left / upper[i, i]
    grown = [sizes[j + 1] / sizes[j] for j in range(ITERS)]
    zero = jnp.zeros((1, 1), jnp.float32)

    target = [upper[0, 0]] + [zero] * ITERS
    rotations = []
    columns = []
    for j in range(ITERS):
        column = [
            upper.get((i, j), zero) + grown[j] * upper[i, j + 1] for i in range(j + 2)
        ]
        for i in range(j):
            cosine, sine = rotations[i]
            column[i], column[i + 1] = (
                cosine * column[i] + sine * column[i + 1],
                cosine * column[i + 1] - sine * column[i],
            )
        radius = jnp.sqrt(column[j] * column[j] + column[j + 1] * column[j + 1])
        cosine, sine = column[j] / radius, column[j + 1] / radius
        rotations.append((cosine, sine))
        column[j] = radius
        target[j + 1] = -sine * target[j]
        target[j] = cosine * target[j]
        columns.append(column)
    solved = [None] * ITERS
    for i in reversed(range(ITERS)):
        left = target[i]
        for j in range(i + 1, ITERS):
            left = left - columns[j][i] * solved[j]
        solved[i] = left / columns[i][i]
    out_held[0, 0, nz : nz + 1, :] = jnp.broadcast_to(
        jnp.abs(target[ITERS]) / upper[0, 0], (1, BLK)
    )
    update = solved[0] * (dirs[0] * (1.0 / DOWN))
    for j in range(1, ITERS):
        update = update + solved[j] * (dirs[j] * (sizes[0] / DOWN / sizes[j]))
    for e in range(nz):
        for v in range(NV):
            out_held[0, 0, e : e + 1, v * NP : (v + 1) * NP] = update[
                v : v + 1, e * NP : (e + 1) * NP
            ]
    stores = [
        pltpu.make_async_copy(out_held, out, out_sem.at[0]),
    ]
    for store in stores:
        store.start()
    for store in stores:
        store.wait()


def solution(mesh):
    nx, ny = mesh.shape["gx"], mesh.shape["gy"]

    def body(rhs, vol_jac, inv_step, face_jac, orientation):
        nz = rhs.shape[2]
        width = nz * NP
        face = jnp.transpose(face_jac[0, 0], (2, 3, 0, 1))
        f32 = jnp.float32
        vmem = pl.BlockSpec(memory_space=pltpu.VMEM)
        dma = pltpu.SemaphoreType.DMA
        result = pl.pallas_call(
            lambda *refs: kernel(nx, ny, nz, *refs),
            out_shape=jax.ShapeDtypeStruct((1, 1, nz + 1, BLK), f32),
            in_specs=[pl.BlockSpec(memory_space=pltpu.HBM)] * 5,
            out_specs=pl.BlockSpec(memory_space=pl.ANY),
            scratch_shapes=[
                pltpu.VMEM((nz, NV * NP, NV * NP), f32),
                pltpu.VMEM(rhs.shape, f32),
                pltpu.VMEM(face.shape, f32),
                pltpu.SMEM(inv_step.shape, f32),
                pltpu.SMEM(orientation.shape, jnp.int32),
                pltpu.VMEM((nz // 2, NV, NV * NP, 2 * NP), f32),
                pltpu.VMEM((NV * 8, FACES * nz), f32),
                pltpu.VMEM((NV * 8, AXES * width), f32),
                pltpu.VMEM((NV * 8, width), f32),
                pltpu.VMEM((8, AXES * width), jnp.int32),
                pltpu.VMEM((8, width), f32),
                pltpu.VMEM((ITERS + 1, 8, width), f32),
                pltpu.VMEM((ITERS, 8, width), f32),
                pltpu.VMEM((ITERS, 4, 8, width), f32),
                pltpu.VMEM((nx * ny, 1, 6 * NP), f32),
                pltpu.VMEM((nz // 2, NV, NV * NP, 2 * NP), f32),
                pltpu.VMEM((nz // 2, NV, NV * NP, 2 * NP), f32),
                pltpu.VMEM((nz // 2, NV, NV * NP, 2 * NP), f32),
                pltpu.VMEM((nz // 2, 2 * BLK, 2 * BLK), jnp.bfloat16),
                pltpu.VMEM((nz // 2, 2 * BLK, 2 * BLK), jnp.bfloat16),
                pltpu.VMEM((nz // 2, 2 * BLK, 2 * BLK), jnp.bfloat16),
                pltpu.VMEM((1, 1, nz + 1, BLK), f32),
                dma((nz,)),
                dma((4,)),
                dma((ITERS, 4)),
                dma((ITERS, 4)),
                dma,
                dma,
                dma((1,)),
            ],
            compiler_params=pltpu.CompilerParams(
                collective_id=0, has_side_effects=True, vmem_limit_bytes=GRANT
            ),
            name="newton_step",
        )(
            *[
                pltpu.with_memory_space_constraint(value, pltpu.HBM)
                for value in (vol_jac, rhs, face, inv_step, orientation)
            ]
        )
        return result[:, :, :nz], result[0, 0, nz, 0]

    placed = (
        P("gx", "gy", None, None),
        P("gx", "gy", None, None, None),
        P("gx", "gy", None),
        P("gx", "gy", None, None, None, None),
        P("gx", "gy", None, None),
    )
    return jax.shard_map(
        body,
        mesh=mesh,
        in_specs=placed,
        out_specs=(P("gx", "gy", None, None), P()),
        check_vma=False,
    )
```

```python
import jax
import jax.numpy as jnp
from jax import lax
from jax.experimental import pallas as pl
from jax.experimental.pallas import tpu as pltpu
from jax.sharding import PartitionSpec as P

Q = 4
NV = 5
ITERS = 3
NS_STEPS = 3
NP = Q**3
BLK = NV * NP
FACES = 6
AXES = 3
PENALTY = 4.0
MESH = pl.DeviceIdType.MESH
DOWN = 2.0**-40
TINY = 1e-36
UNROLL = 64
GRANT = 24 * 2**20


def iota(shape, dim):
    return lax.broadcasted_iota(jnp.int32, shape, dim)


def axis_coords(node, axis):
    first, second, third = node % Q, node // Q % Q, node // (Q * Q)
    pair = [(second, third), (first, third), (first, second)][axis]
    return [first, second, third][axis], pair[0], pair[1]


def node_of(axis, fixed, one, two):
    first, second, third = [(fixed, one, two), (one, fixed, two), (one, two, fixed)][axis]
    return first + Q * second + Q * Q * third


def kernel(
    nx, ny, nz,
    vol, rhs_in, face_in, step_in, orient_in,
    out,
    held_vol, rhs, face, inv_step, orient, factor, aux, wts, own, turn, dinv, basis, dirs, halo, packed,
    square, series, fourth, left_op, right_op, right_two,
    out_held,
    vol_sem, small_sem, halo_send, halo_recv, sum_send, sum_recv, out_sem,
):
    gx, gy = lax.axis_index("gx"), lax.axis_index("gy")
    devices = nx * ny
    width = nz * NP
    pairs = nz // 2
    sides = 3 if ny == 2 else 4
    lanes = 2 * NP
    me = gx * ny + gy
    loads = [
        pltpu.make_async_copy(vol.at[0, 0, e], held_vol.at[e], vol_sem.at[e]) for e in range(nz)
    ]
    small = [
        pltpu.make_async_copy(source, target, small_sem.at[at])
        for at, (source, target) in enumerate(
            [(face_in, face), (orient_in, orient), (step_in, inv_step), (rhs_in, rhs)]
        )
    ]
    for load in small:
        load.start()
    for load in loads:
        load.start()

    def other(along, across):
        return lax.rem(gx + along, nx), lax.rem(gy + across, ny)

    def each_other(visit):
        if devices <= UNROLL:
            for step in range(1, devices):
                visit(step // ny, step % ny)
        else:
            def several(step, carry):
                visit(step // ny, step % ny)
                return carry

            lax.fori_loop(1, devices, several, 0)

    barrier = pltpu.get_barrier_semaphore()

    def greet(along, across):
        pl.semaphore_signal(barrier, inc=1, device_id=other(along, across), device_id_type=MESH)

    each_other(greet)

    node = iota((1, width), 1) % NP
    element = iota((1, width), 1) // NP
    row = iota((FACES * nz, width), 0)
    spreads = []
    covers = []
    for axis in range(AXES):
        fixed = axis_coords(node, axis)[0]
        covered = (fixed == 0) | (fixed == Q - 1)
        covers.append(covered)
        wanted = element * FACES + 2 * axis + jnp.where(fixed == 0, 0, 1)
        spreads.append(jnp.where(covered & (row == wanted), 1.0, 0.0).astype(jnp.float32))
    spread = jnp.concatenate(spreads, axis=1)
    aux[...] = jnp.zeros_like(aux)
    basis[...] = jnp.zeros_like(basis)

    for load in small:
        load.wait()
    for e in range(nz):
        for v in range(NV):
            basis[0, v : v + 1, e * NP : (e + 1) * NP] = (
                rhs[0, 0, e : e + 1, v * NP : (v + 1) * NP] * DOWN
            )
    for e in range(nz):
        for v in range(NV):
            aux[v * 8 : v * 8 + NV, e * FACES : (e + 1) * FACES] = face[:, v, e, :]
    line = iota((NV * 8, width), 0)
    same = jnp.where(line // 8 == line % 8, 1.0, 0.0).astype(jnp.float32)
    step_row = jnp.zeros((1, width), jnp.float32)
    for e in range(nz):
        step_row = jnp.where(element == e, inv_step[0, 0, e], step_row)
    own_part = same * step_row
    expanded = jnp.dot(
        aux[...], spread, precision=lax.Precision.HIGHEST, preferred_element_type=jnp.float32
    )
    for axis in range(AXES):
        at = slice(axis * width, (axis + 1) * width)
        half = 0.5 * expanded[:, at]
        jump = jnp.where(covers[axis], 0.5 * PENALTY * same, 0.0)
        wts[:, at] = half - jump
        own_part = own_part + (half + jump)
        fixed, first, second = axis_coords(node, axis)
        code = jnp.zeros((1, width), jnp.int32)
        for e in range(nz):
            side = jnp.where(fixed == 0, orient[0, 0, e, 2 * axis], orient[0, 0, e, 2 * axis + 1])
            code = jnp.where(element == e, side, code)
        swap, flip_first, flip_second = (code // 4) % 2, code % 2, (code // 2) % 2
        one = first + swap * (second - first)
        two = second + swap * (first - second)
        one = one + flip_first * (Q - 1 - 2 * one)
        two = two + flip_second * (Q - 1 - 2 * two)
        there = jnp.where(covers[axis], node_of(axis, Q - 1 - fixed, one, two), node)
        there = there + (element % 2) * NP
        turn[:, at] = jnp.broadcast_to(there, (8, width))
    own[...] = own_part

    sub = iota((8, lanes), 0)
    low = iota((NP, lanes), 1) < NP
    eye = iota((NP, lanes), 1) % NP == iota((NP, lanes), 0)

    def stack(parts):
        total = jnp.zeros((8, lanes), jnp.float32)
        for v in range(NV):
            total = jnp.where(sub == v, parts[v], total)
        return total

    dinv[...] = jnp.zeros_like(dinv)
    for p in range(pairs):
        at = slice(p * lanes, (p + 1) * lanes)
        loads[2 * p].wait()
        loads[2 * p + 1].wait()
        for w in range(NV):
            cut = slice(w * NP, (w + 1) * NP)

            def tile_of(v):
                rows = slice(v * NP, (v + 1) * NP)
                return jnp.concatenate(
                    [held_vol[2 * p, rows, cut], held_vol[2 * p + 1, rows, cut]], axis=1
                )

            middle = tile_of(w)
            diagonal = jnp.sum(jnp.where(eye, middle, 0.0), axis=0, keepdims=True)
            inverse = 1.0 / (diagonal + own[w * 9 : w * 9 + 1, at])
            dinv[w : w + 1, at] = inverse
            for v in range(NV):
                if v == w:
                    tile = jnp.where(eye, 0.0, middle)
                else:
                    tile = tile_of(v) + jnp.where(eye, own[w * 8 + v : w * 8 + v + 1, at], 0.0)
                factor[p, w, v * NP : (v + 1) * NP, :] = -tile * inverse

    def dense_product(blocks, value, p):
        at = slice(p * lanes, (p + 1) * lanes)
        parts = []
        for v in range(NV):
            total = blocks[p, 0, v * NP : (v + 1) * NP, :] * value[0:1, at]
            for w in range(1, NV):
                total = total + blocks[p, w, v * NP : (v + 1) * NP, :] * value[w : w + 1, at]
            left = jnp.sum(jnp.where(low, total, 0.0), axis=1, keepdims=True)
            right = jnp.sum(jnp.where(low, 0.0, total), axis=1, keepdims=True)
            placed = jnp.where(eye, jnp.where(low, left, right), 0.0)
            parts.append(jnp.sum(placed, axis=0, keepdims=True))
        return stack(parts)

    def power_product(blocks, value):
        return jnp.concatenate([dense_product(blocks, value, p) for p in range(pairs)], axis=1)

    def face_product(axis, before, after):
        fixed = axis_coords(iota((8, width), 1) % NP, axis)[0]
        joined = jnp.where(fixed == Q - 1, before, after)
        pieces = []
        for p in range(pairs):
            at = slice(p * lanes, (p + 1) * lanes)
            here = slice(axis * width + p * lanes, axis * width + (p + 1) * lanes)
            turned = jnp.take_along_axis(
                joined[:, at], turn[:, here], axis=1, mode="promise_in_bounds"
            )
            total = wts[0:8, here] * turned[0:1, :]
            for w in range(1, NV):
                total = total + wts[w * 8 : w * 8 + 8, here] * turned[w : w + 1, :]
            pieces.append(total)
        return jnp.concatenate(pieces, axis=1)

    def put_right(p, v, w, tile, target):
        cut = slice(w * lanes, (w + 1) * lanes)
        upper, lower = slice(v * lanes, v * lanes + NP), slice(v * lanes + NP, (v + 1) * lanes)
        target[p, upper, cut] = jnp.where(low, tile, 0.0).astype(jnp.bfloat16)
        target[p, lower, cut] = jnp.where(low, 0.0, tile).astype(jnp.bfloat16)

    def operands(p):
        for w in range(NV):
            for v in range(NV):
                rows = slice(v * NP, (v + 1) * NP)
                tile = factor[p, w, rows, :]
                left_op[p, rows, w * lanes : (w + 1) * lanes] = tile.astype(jnp.bfloat16)
                put_right(p, v, w, tile, right_op)

    def square_of(p):
        product = jnp.dot(left_op[p, 0:BLK, :], right_op[p], preferred_element_type=jnp.float32)
        for w in range(NV):
            square[p, w] = product[:, w * lanes : (w + 1) * lanes]

    def more_powers():
        for p in range(pairs):
            for w in range(NV):
                for v in range(NV):
                    rows = slice(v * NP, (v + 1) * NP)
                    tile = square[p, w, rows, :]
                    left_op[p, BLK + v * NP : BLK + (v + 1) * NP, w * lanes : (w + 1) * lanes] = (
                        tile.astype(jnp.bfloat16)
                    )
                    put_right(p, v, w, tile, right_two)
        for p in range(pairs):
            both = jnp.dot(left_op[p], right_two[p], preferred_element_type=jnp.float32)
            for w in range(NV):
                cut = slice(w * lanes, (w + 1) * lanes)
                series[p, w] = factor[p, w] + square[p, w] + both[0:BLK, cut]
                fourth[p, w] = both[BLK : 2 * BLK, cut]

    def all_powers():
        for p in range(pairs):
            for w in range(NV):
                cut = slice(w * lanes, (w + 1) * lanes)
                left_op[p, 0:BLK, cut] = fourth[p, w].astype(jnp.bfloat16)
                for v in range(NV):
                    put_right(p, v, w, series[p, w, v * NP : (v + 1) * NP, :], right_op)
        for p in range(pairs):
            last = jnp.dot(left_op[p, 0:BLK, :], right_op[p], preferred_element_type=jnp.float32)
            for w in range(NV):
                cut = slice(w * lanes, (w + 1) * lanes)
                series[p, w] = series[p, w] + (fourth[p, w] + last[:, cut])

    def sum_copy(device):
        return pltpu.make_async_remote_copy(
            src_ref=packed.at[me],
            dst_ref=packed.at[me],
            send_sem=sum_send,
            recv_sem=sum_recv,
            device_id=device,
            device_id_type=MESH,
        )

    def dot(a, b):
        return jnp.sum(jnp.sum(a * b, axis=0, keepdims=True), axis=1, keepdims=True)

    def halo_copy(step, side):
        targets = [
            (lax.rem(gx + 1, nx), gy),
            (lax.rem(gx + nx - 1, nx), gy),
            (gx, lax.rem(gy + 1, ny)),
            (gx, lax.rem(gy + ny - 1, ny)),
        ]
        return pltpu.make_async_remote_copy(
            src_ref=dirs.at[step],
            dst_ref=halo.at[step, side],
            send_sem=halo_send.at[step, side],
            recv_sem=halo_recv.at[step, side],
            device_id=targets[side],
            device_id_type=MESH,
        )

    def apply_jacobian(step, solved, meanwhile):
        direction = dinv[...] * solved
        dirs[step] = direction
        for side in range(sides):
            halo_copy(step, side).start()
        inner_part = (solved - basis[step]) - power_product(factor, solved)
        before, after = pltpu.roll(direction, NP, 1), pltpu.roll(direction, width - NP, 1)
        inner_part = inner_part + face_product(2, before, after)
        meanwhile()
        for side in range(sides):
            halo_copy(step, side).wait()
        basis[step + 1] = (
            inner_part
            + face_product(0, halo[step, 0], halo[step, 1])
            + face_product(1, halo[step, 2], halo[step, sides - 1])
        )

    begun = basis[0]
    solved = begun
    for sweep in range(3):
        solved = begun + power_product(factor, solved)
        for p in range(pairs):
            if sweep == p % 2:
                operands(p)
            if sweep == p % 2 + 1:
                square_of(p)
    solved = solved + power_product(square, power_product(square, solved))
    pl.semaphore_wait(barrier, devices - 1)
    apply_jacobian(0, solved, more_powers)

    solved = basis[1]
    solved = solved + power_product(series, solved)
    solved = solved + power_product(fourth, solved)
    apply_jacobian(1, solved, all_powers)

    solved = basis[2]
    solved = solved + power_product(series, solved)

    count = ITERS + 1
    where = iota((1, lanes), 1)
    zeros = jnp.zeros((1, lanes), jnp.float32)
    slots = {}
    for j in range(count):
        for i in range(j + 1):
            slots[i, j] = len(slots)
    peaks = []
    scaled = []
    rows = [zeros, zeros, zeros]

    def add_products(j):
        vector = basis[j]
        peak = jnp.max(jnp.max(jnp.abs(vector), axis=0, keepdims=True), axis=1, keepdims=True)
        peaks.append(peak)
        scaled.append(vector * jnp.where(peak > TINY, 1.0 / jnp.maximum(peak, TINY), 0.0))
        for i in range(j + 1):
            chosen = where == slots[i, j]
            for at, entry in enumerate([dot(scaled[i], scaled[j]), peaks[i], peaks[j]]):
                rows[at] = jnp.where(chosen, entry, rows[at])

    apply_jacobian(ITERS - 1, solved, lambda: [add_products(j) for j in range(ITERS)])
    add_products(ITERS)
    row, row_peak, column_peak = rows
    packed[me, :, 0:lanes] = row
    packed[me, :, lanes : 2 * lanes] = row_peak
    packed[me, :, 2 * lanes : 3 * lanes] = column_peak

    each_other(lambda along, across: sum_copy(other(along, across)).start())
    arrived = packed.at[pl.ds(0, devices - 1)]
    pltpu.make_async_copy(arrived, arrived, sum_recv).wait()
    pltpu.make_async_copy(arrived, arrived, sum_send).wait()
    row_peaks = packed[:, :, lanes : 2 * lanes]
    column_peaks = packed[:, :, 2 * lanes : 3 * lanes]
    row_peak = jnp.max(row_peaks, axis=0)
    column_peak = jnp.max(column_peaks, axis=0)
    shares = (row_peaks * (1.0 / jnp.maximum(row_peak, TINY))) * (
        column_peaks * (1.0 / jnp.maximum(column_peak, TINY))
    )
    row = jnp.sum(packed[:, :, 0:lanes] * shares, axis=0)
    gram = {key: row[:, at : at + 1] for key, at in slots.items()}
    sizes = [row_peak[:, slots[i, i] : slots[i, i] + 1] for i in range(count)]
    upper = {}
    for i in range(count):
        for j in range(i, count):
            left = gram[i, j]
            for k in range(i):
                left = left - upper[k, i] * upper[k, j]
            upper[i, j] = jnp.sqrt(jnp.maximum(left, 0.0)) if i == j else left / upper[i, i]
    grown = [sizes[j + 1] / sizes[j] for j in range(ITERS)]
    zero = jnp.zeros((1, 1), jnp.float32)

    target = [upper[0, 0]] + [zero] * ITERS
    rotations = []
    columns = []
    for j in range(ITERS):
        column = [
            upper.get((i, j), zero) + grown[j] * upper[i, j + 1] for i in range(j + 2)
        ]
        for i in range(j):
            cosine, sine = rotations[i]
            column[i], column[i + 1] = (
                cosine * column[i] + sine * column[i + 1],
                cosine * column[i + 1] - sine * column[i],
            )
        radius = jnp.sqrt(column[j] * column[j] + column[j + 1] * column[j + 1])
        cosine, sine = column[j] / radius, column[j + 1] / radius
        rotations.append((cosine, sine))
        column[j] = radius
        target[j + 1] = -sine * target[j]
        target[j] = cosine * target[j]
        columns.append(column)
    solved = [None] * ITERS
    for i in reversed(range(ITERS)):
        left = target[i]
        for j in range(i + 1, ITERS):
            left = left - columns[j][i] * solved[j]
        solved[i] = left / columns[i][i]
    out_held[0, 0, nz : nz + 1, :] = jnp.broadcast_to(
        jnp.abs(target[ITERS]) / upper[0, 0], (1, BLK)
    )
    update = solved[0] * (dirs[0] * (1.0 / DOWN))
    for j in range(1, ITERS):
        update = update + solved[j] * (dirs[j] * (sizes[0] / DOWN / sizes[j]))
    for e in range(nz):
        for v in range(NV):
            out_held[0, 0, e : e + 1, v * NP : (v + 1) * NP] = update[
                v : v + 1, e * NP : (e + 1) * NP
            ]
    stores = [
        pltpu.make_async_copy(out_held, out, out_sem.at[0]),
    ]
    for store in stores:
        store.start()
    for store in stores:
        store.wait()


def hand_out(nz, both, update, ratio):
    update[...] = both[:, :, 0:nz, :]
    ratio[...] = both[0, 0, nz : nz + 1, 0:1]


def solution(mesh):
    nx, ny = mesh.shape["gx"], mesh.shape["gy"]

    def body(rhs, vol_jac, inv_step, face_jac, orientation):
        nz = rhs.shape[2]
        width = nz * NP
        face = jnp.transpose(face_jac[0, 0], (2, 3, 0, 1))
        f32 = jnp.float32
        vmem = pl.BlockSpec(memory_space=pltpu.VMEM)
        dma = pltpu.SemaphoreType.DMA
        result = pl.pallas_call(
            lambda *refs: kernel(nx, ny, nz, *refs),
            out_shape=jax.ShapeDtypeStruct((1, 1, nz + 1, BLK), f32),
            in_specs=[pl.BlockSpec(memory_space=pltpu.HBM)] * 5,
            out_specs=pl.BlockSpec(memory_space=pl.ANY),
            scratch_shapes=[
                pltpu.VMEM((nz, NV * NP, NV * NP), f32),
                pltpu.VMEM(rhs.shape, f32),
                pltpu.VMEM(face.shape, f32),
                pltpu.SMEM(inv_step.shape, f32),
                pltpu.SMEM(orientation.shape, jnp.int32),
                pltpu.VMEM((nz // 2, NV, NV * NP, 2 * NP), f32),
                pltpu.VMEM((NV * 8, FACES * nz), f32),
                pltpu.VMEM((NV * 8, AXES * width), f32),
                pltpu.VMEM((NV * 8, width), f32),
                pltpu.VMEM((8, AXES * width), jnp.int32),
                pltpu.VMEM((8, width), f32),
                pltpu.VMEM((ITERS + 1, 8, width), f32),
                pltpu.VMEM((ITERS, 8, width), f32),
                pltpu.VMEM((ITERS, 4, 8, width), f32),
                pltpu.VMEM((nx * ny, 1, 6 * NP), f32),
                pltpu.VMEM((nz // 2, NV, NV * NP, 2 * NP), f32),
                pltpu.VMEM((nz // 2, NV, NV * NP, 2 * NP), f32),
                pltpu.VMEM((nz // 2, NV, NV * NP, 2 * NP), f32),
                pltpu.VMEM((nz // 2, 2 * BLK, 2 * BLK), jnp.bfloat16),
                pltpu.VMEM((nz // 2, 2 * BLK, 2 * BLK), jnp.bfloat16),
                pltpu.VMEM((nz // 2, 2 * BLK, 2 * BLK), jnp.bfloat16),
                pltpu.VMEM((1, 1, nz + 1, BLK), f32),
                dma((nz,)),
                dma((4,)),
                dma((ITERS, 4)),
                dma((ITERS, 4)),
                dma,
                dma,
                dma((1,)),
            ],
            compiler_params=pltpu.CompilerParams(
                collective_id=0, has_side_effects=True, vmem_limit_bytes=GRANT
            ),
            name="newton_step",
        )(
            *[
                pltpu.with_memory_space_constraint(value, pltpu.HBM)
                for value in (vol_jac, rhs, face, inv_step, orientation)
            ]
        )
        update, ratio = pl.pallas_call(
            lambda both, first, second: hand_out(nz, both, first, second),
            out_shape=(
                jax.ShapeDtypeStruct(rhs.shape, f32),
                jax.ShapeDtypeStruct((1, 1), f32),
            ),
            in_specs=[vmem],
            out_specs=(vmem, vmem),
            compiler_params=pltpu.CompilerParams(vmem_limit_bytes=2**20),
            name="hand_out",
        )(result)
        return update, ratio[0, 0]

    placed = (
        P("gx", "gy", None, None),
        P("gx", "gy", None, None, None),
        P("gx", "gy", None),
        P("gx", "gy", None, None, None, None),
        P("gx", "gy", None, None),
    )
    return jax.shard_map(
        body,
        mesh=mesh,
        in_specs=placed,
        out_specs=(P("gx", "gy", None, None), P()),
        check_vma=False,
    )
```

```python
import jax
import jax.numpy as jnp
from jax import lax
from jax.experimental import pallas as pl
from jax.experimental.pallas import tpu as pltpu
from jax.sharding import PartitionSpec as P

Q = 4
NV = 5
ITERS = 3
NS_STEPS = 3
NP = Q**3
BLK = NV * NP
FACES = 6
AXES = 3
PENALTY = 4.0
MESH = pl.DeviceIdType.MESH
DOWN = 2.0**-40
TINY = 1e-36
UNROLL = 64
GRANT = 24 * 2**20


def iota(shape, dim):
    return lax.broadcasted_iota(jnp.int32, shape, dim)


def axis_coords(node, axis):
    first, second, third = node % Q, node // Q % Q, node // (Q * Q)
    pair = [(second, third), (first, third), (first, second)][axis]
    return [first, second, third][axis], pair[0], pair[1]


def node_of(axis, fixed, one, two):
    first, second, third = [(fixed, one, two), (one, fixed, two), (one, two, fixed)][axis]
    return first + Q * second + Q * Q * third


def kernel(
    nx, ny, nz,
    vol, rhs_in, face_in, step_in, orient_in,
    out,
    held_vol, rhs, face, inv_step, orient, factor, aux, wts, own, turn, dinv, basis, dirs, halo, packed,
    square, series, fourth, left_op, right_op, right_two,
    out_held,
    vol_sem, small_sem, halo_send, halo_recv, sum_send, sum_recv, out_sem,
):
    gx, gy = lax.axis_index("gx"), lax.axis_index("gy")
    devices = nx * ny
    width = nz * NP
    pairs = nz // 2
    sides = 3 if ny == 2 else 4
    lanes = 2 * NP
    me = gx * ny + gy
    loads = [
        pltpu.make_async_copy(vol.at[0, 0, e], held_vol.at[e], vol_sem.at[e]) for e in range(nz)
    ]
    small = [
        pltpu.make_async_copy(source, target, small_sem.at[at])
        for at, (source, target) in enumerate(
            [(face_in, face), (orient_in, orient), (step_in, inv_step), (rhs_in, rhs)]
        )
    ]
    for load in small:
        load.start()
    for load in loads:
        load.start()

    def other(along, across):
        return lax.rem(gx + along, nx), lax.rem(gy + across, ny)

    def each_other(visit):
        if devices <= UNROLL:
            for step in range(1, devices):
                visit(step // ny, step % ny)
        else:
            def several(step, carry):
                visit(step // ny, step % ny)
                return carry

            lax.fori_loop(1, devices, several, 0)

    barrier = pltpu.get_barrier_semaphore()

    def greet(along, across):
        pl.semaphore_signal(barrier, inc=1, device_id=other(along, across), device_id_type=MESH)

    each_other(greet)

    node = iota((1, width), 1) % NP
    element = iota((1, width), 1) // NP
    row = iota((FACES * nz, width), 0)
    spreads = []
    covers = []
    for axis in range(AXES):
        fixed = axis_coords(node, axis)[0]
        covered = (fixed == 0) | (fixed == Q - 1)
        covers.append(covered)
        wanted = element * FACES + 2 * axis + jnp.where(fixed == 0, 0, 1)
        spreads.append(jnp.where(covered & (row == wanted), 1.0, 0.0).astype(jnp.float32))
    spread = jnp.concatenate(spreads, axis=1)
    aux[...] = jnp.zeros_like(aux)
    basis[...] = jnp.zeros_like(basis)

    for load in small:
        load.wait()
    for e in range(nz):
        for v in range(NV):
            basis[0, v : v + 1, e * NP : (e + 1) * NP] = (
                rhs[0, 0, e : e + 1, v * NP : (v + 1) * NP] * DOWN
            )
    for e in range(nz):
        for v in range(NV):
            aux[v * 8 : v * 8 + NV, e * FACES : (e + 1) * FACES] = face[:, v, e, :]
    line = iota((NV * 8, width), 0)
    same = jnp.where(line // 8 == line % 8, 1.0, 0.0).astype(jnp.float32)
    step_row = jnp.zeros((1, width), jnp.float32)
    for e in range(nz):
        step_row = jnp.where(element == e, inv_step[0, 0, e], step_row)
    own_part = same * step_row
    expanded = jnp.dot(
        aux[...], spread, precision=lax.Precision.HIGHEST, preferred_element_type=jnp.float32
    )
    for axis in range(AXES):
        at = slice(axis * width, (axis + 1) * width)
        half = 0.5 * expanded[:, at]
        jump = jnp.where(covers[axis], 0.5 * PENALTY * same, 0.0)
        wts[:, at] = half - jump
        own_part = own_part + (half + jump)
        fixed, first, second = axis_coords(node, axis)
        code = jnp.zeros((1, width), jnp.int32)
        for e in range(nz):
            side = jnp.where(fixed == 0, orient[0, 0, e, 2 * axis], orient[0, 0, e, 2 * axis + 1])
            code = jnp.where(element == e, side, code)
        swap, flip_first, flip_second = (code // 4) % 2, code % 2, (code // 2) % 2
        one = first + swap * (second - first)
        two = second + swap * (first - second)
        one = one + flip_first * (Q - 1 - 2 * one)
        two = two + flip_second * (Q - 1 - 2 * two)
        there = jnp.where(covers[axis], node_of(axis, Q - 1 - fixed, one, two), node)
        there = there + (element % 2) * NP
        turn[:, at] = jnp.broadcast_to(there, (8, width))
    own[...] = own_part

    sub = iota((8, lanes), 0)
    low = iota((NP, lanes), 1) < NP
    eye = iota((NP, lanes), 1) % NP == iota((NP, lanes), 0)

    def stack(parts):
        total = jnp.zeros((8, lanes), jnp.float32)
        for v in range(NV):
            total = jnp.where(sub == v, parts[v], total)
        return total

    dinv[...] = jnp.zeros_like(dinv)
    for p in range(pairs):
        at = slice(p * lanes, (p + 1) * lanes)
        loads[2 * p].wait()
        loads[2 * p + 1].wait()
        for w in range(NV):
            cut = slice(w * NP, (w + 1) * NP)

            def tile_of(v):
                rows = slice(v * NP, (v + 1) * NP)
                return jnp.concatenate(
                    [held_vol[2 * p, rows, cut], held_vol[2 * p + 1, rows, cut]], axis=1
                )

            middle = tile_of(w)
            diagonal = jnp.sum(jnp.where(eye, middle, 0.0), axis=0, keepdims=True)
            inverse = 1.0 / (diagonal + own[w * 9 : w * 9 + 1, at])
            dinv[w : w + 1, at] = inverse
            for v in range(NV):
                if v == w:
                    tile = jnp.where(eye, 0.0, middle)
                else:
                    tile = tile_of(v) + jnp.where(eye, own[w * 8 + v : w * 8 + v + 1, at], 0.0)
                factor[p, w, v * NP : (v + 1) * NP, :] = -tile * inverse

    def dense_product(blocks, value, p):
        at = slice(p * lanes, (p + 1) * lanes)
        parts = []
        for v in range(NV):
            total = blocks[p, 0, v * NP : (v + 1) * NP, :] * value[0:1, at]
            for w in range(1, NV):
                total = total + blocks[p, w, v * NP : (v + 1) * NP, :] * value[w : w + 1, at]
            left = jnp.sum(jnp.where(low, total, 0.0), axis=1, keepdims=True)
            right = jnp.sum(jnp.where(low, 0.0, total), axis=1, keepdims=True)
            placed = jnp.where(eye, jnp.where(low, left, right), 0.0)
            parts.append(jnp.sum(placed, axis=0, keepdims=True))
        return stack(parts)

    def power_product(blocks, value):
        return jnp.concatenate([dense_product(blocks, value, p) for p in range(pairs)], axis=1)

    def face_product(axis, before, after):
        fixed = axis_coords(iota((8, width), 1) % NP, axis)[0]
        joined = jnp.where(fixed == Q - 1, before, after)
        pieces = []
        for p in range(pairs):
            at = slice(p * lanes, (p + 1) * lanes)
            here = slice(axis * width + p * lanes, axis * width + (p + 1) * lanes)
            turned = jnp.take_along_axis(
                joined[:, at], turn[:, here], axis=1, mode="promise_in_bounds"
            )
            total = wts[0:8, here] * turned[0:1, :]
            for w in range(1, NV):
                total = total + wts[w * 8 : w * 8 + 8, here] * turned[w : w + 1, :]
            pieces.append(total)
        return jnp.concatenate(pieces, axis=1)

    def put_right(p, v, w, tile, target):
        cut = slice(w * lanes, (w + 1) * lanes)
        upper, lower = slice(v * lanes, v * lanes + NP), slice(v * lanes + NP, (v + 1) * lanes)
        target[p, upper, cut] = jnp.where(low, tile, 0.0).astype(jnp.bfloat16)
        target[p, lower, cut] = jnp.where(low, 0.0, tile).astype(jnp.bfloat16)

    def operands(p):
        for w in range(NV):
            for v in range(NV):
                rows = slice(v * NP, (v + 1) * NP)
                tile = factor[p, w, rows, :]
                left_op[p, rows, w * lanes : (w + 1) * lanes] = tile.astype(jnp.bfloat16)
                put_right(p, v, w, tile, right_op)

    def square_of(p):
        product = jnp.dot(left_op[p, 0:BLK, :], right_op[p], preferred_element_type=jnp.float32)
        for w in range(NV):
            square[p, w] = product[:, w * lanes : (w + 1) * lanes]

    def more_powers():
        for p in range(pairs):
            for w in range(NV):
                for v in range(NV):
                    rows = slice(v * NP, (v + 1) * NP)
                    tile = square[p, w, rows, :]
                    left_op[p, BLK + v * NP : BLK + (v + 1) * NP, w * lanes : (w + 1) * lanes] = (
                        tile.astype(jnp.bfloat16)
                    )
                    put_right(p, v, w, tile, right_two)
        for p in range(pairs):
            both = jnp.dot(left_op[p], right_two[p], preferred_element_type=jnp.float32)
            for w in range(NV):
                cut = slice(w * lanes, (w + 1) * lanes)
                series[p, w] = factor[p, w] + square[p, w] + both[0:BLK, cut]
                fourth[p, w] = both[BLK : 2 * BLK, cut]

    def all_powers():
        for p in range(pairs):
            for w in range(NV):
                cut = slice(w * lanes, (w + 1) * lanes)
                left_op[p, 0:BLK, cut] = fourth[p, w].astype(jnp.bfloat16)
                for v in range(NV):
                    put_right(p, v, w, series[p, w, v * NP : (v + 1) * NP, :], right_op)
        for p in range(pairs):
            last = jnp.dot(left_op[p, 0:BLK, :], right_op[p], preferred_element_type=jnp.float32)
            for w in range(NV):
                cut = slice(w * lanes, (w + 1) * lanes)
                series[p, w] = series[p, w] + (fourth[p, w] + last[:, cut])

    def sum_copy(device):
        return pltpu.make_async_remote_copy(
            src_ref=packed.at[me],
            dst_ref=packed.at[me],
            send_sem=sum_send,
            recv_sem=sum_recv,
            device_id=device,
            device_id_type=MESH,
        )

    def dot(a, b):
        return jnp.sum(jnp.sum(a * b, axis=0, keepdims=True), axis=1, keepdims=True)

    def halo_copy(step, side):
        targets = [
            (lax.rem(gx + 1, nx), gy),
            (lax.rem(gx + nx - 1, nx), gy),
            (gx, lax.rem(gy + 1, ny)),
            (gx, lax.rem(gy + ny - 1, ny)),
        ]
        return pltpu.make_async_remote_copy(
            src_ref=dirs.at[step],
            dst_ref=halo.at[step, side],
            send_sem=halo_send.at[step, side],
            recv_sem=halo_recv.at[step, side],
            device_id=targets[side],
            device_id_type=MESH,
        )

    def apply_jacobian(step, solved, meanwhile):
        direction = dinv[...] * solved
        dirs[step] = direction
        for side in range(sides):
            halo_copy(step, side).start()
        inner_part = (solved - basis[step]) - power_product(factor, solved)
        before, after = pltpu.roll(direction, NP, 1), pltpu.roll(direction, width - NP, 1)
        inner_part = inner_part + face_product(2, before, after)
        meanwhile()
        for side in range(sides):
            halo_copy(step, side).wait()
        basis[step + 1] = (
            inner_part
            + face_product(0, halo[step, 0], halo[step, 1])
            + face_product(1, halo[step, 2], halo[step, sides - 1])
        )

    begun = basis[0]
    solved = begun
    for sweep in range(3):
        solved = begun + power_product(factor, solved)
        for p in range(pairs):
            if sweep == p % 2:
                operands(p)
            if sweep == p % 2 + 1:
                square_of(p)
    solved = solved + power_product(square, power_product(square, solved))
    pl.semaphore_wait(barrier, devices - 1)
    apply_jacobian(0, solved, lambda: [more_powers(), all_powers()])

    solved = basis[1]
    solved = solved + power_product(series, solved)
    apply_jacobian(1, solved, lambda: None)

    solved = basis[2]
    solved = solved + power_product(series, solved)

    count = ITERS + 1
    where = iota((1, lanes), 1)
    zeros = jnp.zeros((1, lanes), jnp.float32)
    slots = {}
    for j in range(count):
        for i in range(j + 1):
            slots[i, j] = len(slots)
    peaks = []
    scaled = []
    rows = [zeros, zeros, zeros]

    def add_products(j):
        vector = basis[j]
        peak = jnp.max(jnp.max(jnp.abs(vector), axis=0, keepdims=True), axis=1, keepdims=True)
        peaks.append(peak)
        scaled.append(vector * jnp.where(peak > TINY, 1.0 / jnp.maximum(peak, TINY), 0.0))
        for i in range(j + 1):
            chosen = where == slots[i, j]
            for at, entry in enumerate([dot(scaled[i], scaled[j]), peaks[i], peaks[j]]):
                rows[at] = jnp.where(chosen, entry, rows[at])

    apply_jacobian(ITERS - 1, solved, lambda: [add_products(j) for j in range(ITERS)])
    add_products(ITERS)
    row, row_peak, column_peak = rows
    packed[me, :, 0:lanes] = row
    packed[me, :, lanes : 2 * lanes] = row_peak
    packed[me, :, 2 * lanes : 3 * lanes] = column_peak

    each_other(lambda along, across: sum_copy(other(along, across)).start())
    arrived = packed.at[pl.ds(0, devices - 1)]
    pltpu.make_async_copy(arrived, arrived, sum_recv).wait()
    pltpu.make_async_copy(arrived, arrived, sum_send).wait()
    row_peaks = packed[:, :, lanes : 2 * lanes]
    column_peaks = packed[:, :, 2 * lanes : 3 * lanes]
    row_peak = jnp.max(row_peaks, axis=0)
    column_peak = jnp.max(column_peaks, axis=0)
    shares = (row_peaks * (1.0 / jnp.maximum(row_peak, TINY))) * (
        column_peaks * (1.0 / jnp.maximum(column_peak, TINY))
    )
    row = jnp.sum(packed[:, :, 0:lanes] * shares, axis=0)
    gram = {key: row[:, at : at + 1] for key, at in slots.items()}
    sizes = [row_peak[:, slots[i, i] : slots[i, i] + 1] for i in range(count)]
    upper = {}
    for i in range(count):
        for j in range(i, count):
            left = gram[i, j]
            for k in range(i):
                left = left - upper[k, i] * upper[k, j]
            upper[i, j] = jnp.sqrt(jnp.maximum(left, 0.0)) if i == j else left / upper[i, i]
    grown = [sizes[j + 1] / sizes[j] for j in range(ITERS)]
    zero = jnp.zeros((1, 1), jnp.float32)

    target = [upper[0, 0]] + [zero] * ITERS
    rotations = []
    columns = []
    for j in range(ITERS):
        column = [
            upper.get((i, j), zero) + grown[j] * upper[i, j + 1] for i in range(j + 2)
        ]
        for i in range(j):
            cosine, sine = rotations[i]
            column[i], column[i + 1] = (
                cosine * column[i] + sine * column[i + 1],
                cosine * column[i + 1] - sine * column[i],
            )
        radius = jnp.sqrt(column[j] * column[j] + column[j + 1] * column[j + 1])
        cosine, sine = column[j] / radius, column[j + 1] / radius
        rotations.append((cosine, sine))
        column[j] = radius
        target[j + 1] = -sine * target[j]
        target[j] = cosine * target[j]
        columns.append(column)
    solved = [None] * ITERS
    for i in reversed(range(ITERS)):
        left = target[i]
        for j in range(i + 1, ITERS):
            left = left - columns[j][i] * solved[j]
        solved[i] = left / columns[i][i]
    out_held[0, 0, nz : nz + 1, :] = jnp.broadcast_to(
        jnp.abs(target[ITERS]) / upper[0, 0], (1, BLK)
    )
    update = solved[0] * (dirs[0] * (1.0 / DOWN))
    for j in range(1, ITERS):
        update = update + solved[j] * (dirs[j] * (sizes[0] / DOWN / sizes[j]))
    for e in range(nz):
        for v in range(NV):
            out_held[0, 0, e : e + 1, v * NP : (v + 1) * NP] = update[
                v : v + 1, e * NP : (e + 1) * NP
            ]
    stores = [
        pltpu.make_async_copy(out_held, out, out_sem.at[0]),
    ]
    for store in stores:
        store.start()
    for store in stores:
        store.wait()


def hand_out(nz, both, update, ratio):
    update[...] = both[:, :, 0:nz, :]
    ratio[...] = both[0, 0, nz : nz + 1, 0:1]


def solution(mesh):
    nx, ny = mesh.shape["gx"], mesh.shape["gy"]

    def body(rhs, vol_jac, inv_step, face_jac, orientation):
        nz = rhs.shape[2]
        width = nz * NP
        face = jnp.transpose(face_jac[0, 0], (2, 3, 0, 1))
        f32 = jnp.float32
        vmem = pl.BlockSpec(memory_space=pltpu.VMEM)
        dma = pltpu.SemaphoreType.DMA
        result = pl.pallas_call(
            lambda *refs: kernel(nx, ny, nz, *refs),
            out_shape=jax.ShapeDtypeStruct((1, 1, nz + 1, BLK), f32),
            in_specs=[pl.BlockSpec(memory_space=pltpu.HBM)] * 5,
            out_specs=pl.BlockSpec(memory_space=pl.ANY),
            scratch_shapes=[
                pltpu.VMEM((nz, NV * NP, NV * NP), f32),
                pltpu.VMEM(rhs.shape, f32),
                pltpu.VMEM(face.shape, f32),
                pltpu.SMEM(inv_step.shape, f32),
                pltpu.SMEM(orientation.shape, jnp.int32),
                pltpu.VMEM((nz // 2, NV, NV * NP, 2 * NP), f32),
                pltpu.VMEM((NV * 8, FACES * nz), f32),
                pltpu.VMEM((NV * 8, AXES * width), f32),
                pltpu.VMEM((NV * 8, width), f32),
                pltpu.VMEM((8, AXES * width), jnp.int32),
                pltpu.VMEM((8, width), f32),
                pltpu.VMEM((ITERS + 1, 8, width), f32),
                pltpu.VMEM((ITERS, 8, width), f32),
                pltpu.VMEM((ITERS, 4, 8, width), f32),
                pltpu.VMEM((nx * ny, 1, 6 * NP), f32),
                pltpu.VMEM((nz // 2, NV, NV * NP, 2 * NP), f32),
                pltpu.VMEM((nz // 2, NV, NV * NP, 2 * NP), f32),
                pltpu.VMEM((nz // 2, NV, NV * NP, 2 * NP), f32),
                pltpu.VMEM((nz // 2, 2 * BLK, 2 * BLK), jnp.bfloat16),
                pltpu.VMEM((nz // 2, 2 * BLK, 2 * BLK), jnp.bfloat16),
                pltpu.VMEM((nz // 2, 2 * BLK, 2 * BLK), jnp.bfloat16),
                pltpu.VMEM((1, 1, nz + 1, BLK), f32),
                dma((nz,)),
                dma((4,)),
                dma((ITERS, 4)),
                dma((ITERS, 4)),
                dma,
                dma,
                dma((1,)),
            ],
            compiler_params=pltpu.CompilerParams(
                collective_id=0, has_side_effects=True, vmem_limit_bytes=GRANT
            ),
            name="newton_step",
        )(
            *[
                pltpu.with_memory_space_constraint(value, pltpu.HBM)
                for value in (vol_jac, rhs, face, inv_step, orientation)
            ]
        )
        update, ratio = pl.pallas_call(
            lambda both, first, second: hand_out(nz, both, first, second),
            out_shape=(
                jax.ShapeDtypeStruct(rhs.shape, f32),
                jax.ShapeDtypeStruct((1, 1), f32),
            ),
            in_specs=[vmem],
            out_specs=(vmem, vmem),
            compiler_params=pltpu.CompilerParams(vmem_limit_bytes=2**20),
            name="hand_out",
        )(result)
        return update, ratio[0, 0]

    placed = (
        P("gx", "gy", None, None),
        P("gx", "gy", None, None, None),
        P("gx", "gy", None),
        P("gx", "gy", None, None, None, None),
        P("gx", "gy", None, None),
    )
    return jax.shard_map(
        body,
        mesh=mesh,
        in_specs=placed,
        out_specs=(P("gx", "gy", None, None), P()),
        check_vma=False,
    )
```
